512 devices in a mesh: dp: 32 (over x, z), expert: 16 (over y, core).
Axes of the slice: x: 4, y: 8, z: 8, core: 2. Of those that a mesh axis runs over, the one named last changes fastest.
Arguments:
- step_inputs: bfloat16 [65536, 2048], P(('dp', 'expert')), may hold values from -6 to 6
- step_cotangent: bfloat16 [65536, 2048], P(('dp', 'expert')), may hold values from -6 to 6
- step_routes: int32 [65536, 1], P(('dp', 'expert')), may hold values from 0 to 3; in each aligned block of 128 rows (0 to 127, 128 to 255, ...) at most 40 rows name the same one
- step_gates: float32 [65536, 1], P(('dp', 'expert')), may hold values from 0.1 to 1
- next_inputs: bfloat16 [65536, 2048], P(('dp', 'expert')), may hold values from -6 to 6
- next_routes: int32 [65536, 1], P(('dp', 'expert')), may hold values from 0 to 3; in each aligned block of 128 rows (0 to 127, 128 to 255, ...) at most 40 rows name the same one
- next_gates: float32 [65536, 1], P(('dp', 'expert')), may hold values from 0.1 to 1
- master_weights: float32 [16, 2048, 864], P('expert', 'dp'), may hold values from -4 to 4
- first_moment: float32 [16, 2048, 864], P('expert', 'dp'), may hold values from -0.6 to 0.6
- second_moment: float32 [16, 2048, 864], P('expert', 'dp'), may hold values from 0.01 to 0.2
- owner_plan: int32 [16], replicated, may hold values from 0 to 15, as said below
Outputs:
- layer_output: bfloat16 [65536, 2048], P(('dp', 'expert'))
- moved_weights: float32 [16, 2048, 864], P('expert', 'dp')
- moved_first: float32 [16, 2048, 864], P('expert', 'dp')
- moved_second: float32 [16, 2048, 864], P('expert', 'dp')
The draws below stay inside these ranges and needn't reach their ends.
Inputs may be any that keep to these rules, and one draw needn't show every extreme that they name: `step_routes`: among the 128 tokens of one device no expert is named more than 40 times. `next_routes`: among the 128 tokens of one device no expert is named more than 40 times. `owner_plan`: every index appears once.
All inputs are finite; a program needn't handle non-finite values.
Results may differ from the reference program's by a relative error of at most 0.025.
Values may be sent and summed in bfloat16 or wider, within the bound.
No kernel may reach another device: no remote copies, remote signals or barrier semaphores. Data moves between devices by JAX's collectives and lax.ppermute only.
A program may use at most 64 MiB of HBM per device.

```python
import math
from functools import partial
import jax
import jax.numpy as jnp
import numpy as np
from jax import lax

D = 2048
HID = 1152
EXPERTS = 4
TOPK = 1
TOK_DEV = 128
SPLIT = 4
HID_DEV = 288
SLABS = 16
CAP = 40
TOKENS = 65536
N_DP = 32
N_EXPERT = 16


def draw_owner_plan(key, part):
    mixed = jax.random.fold_in(key, 7919)
    return jax.random.permutation(mixed, SLABS).astype(jnp.int32)


def levels(key, extent, shards, low, largest):
    factor_of, own = 1.0, jax.random.fold_in(key, 6)
    for axis_at, parts in shards:
        heights = jnp.exp(jax.random.uniform(jax.random.fold_in(own, axis_at), (parts,), jnp.float32, low / len(shards), largest / len(shards)))
        factor_of = factor_of * jnp.repeat(heights, extent[axis_at] // parts).reshape([-1 if axis == axis_at else 1 for axis in range(len(extent))])
    return factor_of


def deal_out(stream_key, own, number, rows, count, top, limit, skew):
    sequence = jax.random.permutation(stream_key, count)
    packed, usual = load_shares(count, rows * top, limit, skew, True), load_shares(count, rows * top, limit, skew, False)
    places = jnp.arange(count)

    def named(tallies, offset_by):
        used = int((tallies > 0).sum())
        fixed = max(1, used // 4)
        shifted = fixed + (places - fixed + offset_by * (used - fixed)) % max(1, count - fixed)
        return jnp.zeros((count,), jnp.int32).at[sequence[jnp.where(places < fixed, places, shifted)]].set(jnp.asarray(tallies, jnp.int32))

    tallies = jnp.where(number % 4 == 0, named(packed, number // 4), named(usual, number - number // 4 - 1))
    mixed = jax.random.permutation(jax.random.fold_in(own, 3), count)
    giver, taker = mixed[0:count // 2 * 2:2], mixed[1:count // 2 * 2:2]
    slack = jnp.minimum(tallies[giver] - 1, limit - tallies[taker]) // 2
    slack = jnp.where((giver == sequence[0]) | (taker == sequence[0]) | (tallies[taker] == 0), 0, jnp.maximum(slack, 0))
    shifted = jax.random.randint(jax.random.fold_in(own, 4), (count // 2,), 0, 1 << 20) % (slack + 1)
    tallies = tallies.at[giver].add(-shifted).at[taker].add(shifted)
    labels = jnp.searchsorted(jnp.cumsum(tallies), jnp.arange(rows * top), side="right").astype(jnp.int32)
    grid = labels.reshape(top, rows).T
    grid = grid[jax.random.permutation(jax.random.fold_in(own, 1), rows)]
    offset_by = jax.random.randint(jax.random.fold_in(own, 2), (rows, 1), 0, top)
    return jnp.take_along_axis(grid, (jnp.arange(top)[None, :] + offset_by) % top, axis=1)


def load_shares(count, total, most, slope, full):
    portions = [(1 << 20) // math.isqrt(rank ** slope) + 1 for rank in range(1, count + 1)]
    largest = most if full else min(most, max(-(-total // count), total * portions[0] // sum(portions)))
    least = 1 if total - largest >= count - 1 else 0
    holding, spare = [largest] + [least] * (count - 1), total - largest - least * (count - 1)
    while spare > 0:
        candidates = [i for i in range(1, count) if holding[i] < largest] or [i for i in range(1, count) if holding[i] < most]
        whole, remaining = sum([portions[i] for i in candidates]), spare
        for i in candidates:
            more = min(most - holding[i], max(1, remaining * portions[i] // whole), spare)
            holding[i] = holding[i] + more
            spare = spare - more
    return np.array(holding)


def gaussian(rng, shape, scale, bound, split=(), kind=jnp.bfloat16):
    drawn = jax.random.normal(rng, shape, jnp.float32) * scale
    if len(split) > 0:
        drawn = levels(rng, shape, split, -0.22, 0.18) * drawn
    return jnp.clip(drawn, min=-bound, max=bound).astype(kind)


def setup_inputs(seed: int = 0) -> dict:
    key_list = jax.random.split(jax.random.key(seed), 12)
    step_inputs = gaussian(key_list[0], (TOKENS, D), 1.0, 6.0, ((0, 512),))
    step_cotangent = gaussian(key_list[1], (TOKENS, D), 1.0, 6.0, ((0, 512),))
    step_routes_keys = jax.random.split(jax.random.fold_in(key_list[2], 1), TOKENS // TOK_DEV)
    step_routes_turns = jax.random.permutation(jax.random.fold_in(key_list[2], 3), TOKENS // TOK_DEV)
    step_routes = jax.vmap(lambda own, number: deal_out(jax.random.fold_in(key_list[2], 2), own, number, TOK_DEV, EXPERTS, TOPK, CAP, 2))(step_routes_keys, step_routes_turns).reshape((TOKENS, TOPK))
    step_gates = jnp.clip(0.1 + 0.9 * jax.random.uniform(key_list[3], (TOKENS, TOPK), jnp.float32) ** levels(key_list[3], (TOKENS, TOPK), ((0, 512),), -0.2, 0.2), 0.1, 1.0)
    next_inputs = gaussian(key_list[4], (TOKENS, D), 1.0, 6.0, ((0, 512),))
    next_routes_keys = jax.random.split(jax.random.fold_in(key_list[5], 1), TOKENS // TOK_DEV)
    next_routes_turns = jax.random.permutation(jax.random.fold_in(key_list[5], 3), TOKENS // TOK_DEV)
    next_routes = jax.vmap(lambda own, number: deal_out(jax.random.fold_in(key_list[5], 2), own, number, TOK_DEV, EXPERTS, TOPK, CAP, 2))(next_routes_keys, next_routes_turns).reshape((TOKENS, TOPK))
    next_gates = jnp.clip(0.1 + 0.9 * jax.random.uniform(key_list[6], (TOKENS, TOPK), jnp.float32) ** levels(key_list[6], (TOKENS, TOPK), ((0, 512),), -0.2, 0.2), 0.1, 1.0)
    master_weights = gaussian(key_list[7], (SLABS, D, 3 * HID_DEV), 1.0, 4.0, ((0, 16), (1, 32)), jnp.float32)
    first_moment = gaussian(key_list[8], (SLABS, D, 3 * HID_DEV), 0.1, 0.6, ((0, 16), (1, 32)), jnp.float32)
    second_moment = jnp.clip(jnp.exp(math.log(0.2) - 2.9957323 * jax.random.uniform(key_list[9], (SLABS, D, 3 * HID_DEV), jnp.float32) ** levels(key_list[9], (SLABS, D, 3 * HID_DEV), ((0, 16), (1, 32)), -0.2, 0.2)), 0.01, 0.2)
    owner_plan = draw_owner_plan(jax.random.fold_in(key_list[11], 71), 0)
    return {"step_inputs": step_inputs, "step_cotangent": step_cotangent, "step_routes": step_routes, "step_gates": step_gates, "next_inputs": next_inputs, "next_routes": next_routes, "next_gates": next_gates, "master_weights": master_weights, "first_moment": first_moment, "second_moment": second_moment, "owner_plan": owner_plan}


beta_one = 0.9
beta_two = 0.95
learn_rate = 0.2
decay_rate = 0.1
adam_step = 10.0
adam_eps = 1e-08

def slot_targets(routes, capacity):
    pair_ids = routes.reshape(-1).astype(jnp.int32)
    one_hot = (pair_ids[:, None] == jnp.arange(EXPERTS, dtype=jnp.int32)[None, :]).astype(jnp.int32)
    earlier = jnp.cumsum(one_hot, axis=0) - one_hot
    slot_ids = lax.optimization_barrier(jnp.sum(earlier * one_hot, axis=1)).astype(jnp.int32)
    return pair_ids * capacity + slot_ids

def dispatch(routes, payload):
    targets = slot_targets(routes, CAP)
    filled = jnp.zeros((EXPERTS * CAP, payload.shape[1]), payload.dtype).at[targets].set(payload)
    return filled.reshape(EXPERTS, CAP, payload.shape[1])

def reference(step_inputs, step_cotangent, step_routes, step_gates, next_inputs, next_routes, next_gates, master_weights, first_moment, second_moment, owner_plan):
    blocks = N_DP * N_EXPERT
    width = HID_DEV
    in_scale = D ** (-0.5)
    out_scale = HID ** (-0.5)
    pair_count = TOK_DEV * TOPK
    step_blocks = step_routes.reshape(blocks, TOK_DEV, TOPK)
    input_pairs = jnp.repeat(step_inputs, TOPK, axis=0).reshape(blocks, pair_count, D)
    scaled_pairs = (jnp.repeat(step_cotangent, TOPK, axis=0).astype(jnp.float32) * step_gates.reshape(-1, 1)).astype(jnp.bfloat16)
    scaled_pairs = scaled_pairs.reshape(blocks, pair_count, D)
    sent_inputs = jax.vmap(dispatch)(step_blocks, input_pairs)
    sent_scaled = jax.vmap(dispatch)(step_blocks, scaled_pairs)
    compute_weights = master_weights.astype(jnp.bfloat16)

    def slab_gradient(slab_index):
        expert = slab_index // SPLIT
        inputs_rows = jnp.take(sent_inputs, expert, axis=1).reshape(-1, D)
        scaled_rows = jnp.take(sent_scaled, expert, axis=1).reshape(-1, D)
        weights = jnp.take(compute_weights, slab_index, axis=0)
        gate_pre = jnp.dot(inputs_rows, weights[:, :width], preferred_element_type=jnp.float32) * in_scale
        up_pre = jnp.dot(inputs_rows, weights[:, width:2 * width], preferred_element_type=jnp.float32) * in_scale
        down_back = jnp.dot(scaled_rows, weights[:, 2 * width:], preferred_element_type=jnp.float32) * out_scale
        sigmoid_gate = jax.nn.sigmoid(gate_pre)
        silu_gate = gate_pre * sigmoid_gate
        activation = (silu_gate * up_pre).astype(jnp.bfloat16)
        gate_grad = (down_back * up_pre * sigmoid_gate * (1.0 + gate_pre * (1.0 - sigmoid_gate))).astype(jnp.bfloat16)
        up_grad = (down_back * silu_gate).astype(jnp.bfloat16)
        inputs_groups = inputs_rows.reshape(N_DP, -1, D).astype(jnp.float32)
        scaled_groups = scaled_rows.reshape(N_DP, -1, D).astype(jnp.float32)
        gate_part = jnp.einsum('nrd,nrh->ndh', inputs_groups, gate_grad.reshape(N_DP, -1, width).astype(jnp.float32), precision=lax.Precision.HIGHEST) * in_scale
        up_part = jnp.einsum('nrd,nrh->ndh', inputs_groups, up_grad.reshape(N_DP, -1, width).astype(jnp.float32), precision=lax.Precision.HIGHEST) * in_scale
        down_part = jnp.einsum('nrd,nrh->ndh', scaled_groups, activation.reshape(N_DP, -1, width).astype(jnp.float32), precision=lax.Precision.HIGHEST) * out_scale
        partial_grad = jnp.concatenate([gate_part, up_part, down_part], axis=2).astype(jnp.bfloat16)
        return lax.optimization_barrier(jnp.sum(partial_grad.astype(jnp.float32), axis=0))
    gradient = lax.map(slab_gradient, jnp.arange(SLABS, dtype=jnp.int32))
    first_new = beta_one * first_moment + (1.0 - beta_one) * gradient
    second_new = beta_two * second_moment + (1.0 - beta_two) * gradient * gradient
    first_hat = first_new / (1.0 - beta_one ** adam_step)
    second_hat = second_new / (1.0 - beta_two ** adam_step)
    weights_new = master_weights - learn_rate * (first_hat / (jnp.sqrt(second_hat) + adam_eps) + decay_rate * master_weights)
    moved_weights = jnp.zeros_like(weights_new).at[owner_plan].set(weights_new)
    moved_first = jnp.zeros_like(first_new).at[owner_plan].set(first_new)
    moved_second = jnp.zeros_like(second_new).at[owner_plan].set(second_new)
    next_blocks = next_routes.reshape(blocks, TOK_DEV, TOPK)
    next_pairs = jnp.repeat(next_inputs, TOPK, axis=0).reshape(blocks, pair_count, D)
    sent_next = jax.vmap(dispatch)(next_blocks, next_pairs)
    next_targets = jax.vmap(partial(slot_targets, capacity=CAP))(next_blocks)
    pair_expert = (next_targets // CAP).reshape(-1)
    pair_rows = (jnp.arange(blocks, dtype=jnp.int32)[:, None] * CAP + next_targets % CAP).reshape(-1).astype(jnp.int32)
    serve_weights = weights_new.astype(jnp.bfloat16)

    def add_slab(running, slab_index):
        expert = slab_index // SPLIT
        weights = jnp.take(serve_weights, slab_index, axis=0)
        rows_in = jnp.take(sent_next, expert, axis=1).reshape(-1, D)
        gate_pre = jnp.dot(rows_in, weights[:, :width], preferred_element_type=jnp.float32) * in_scale
        up_pre = jnp.dot(rows_in, weights[:, width:2 * width], preferred_element_type=jnp.float32) * in_scale
        activation = (gate_pre * jax.nn.sigmoid(gate_pre) * up_pre).astype(jnp.bfloat16)
        slab_partial = (lax.dot_general(activation, weights[:, 2 * width:], (((1,), (1,)), ((), ())), preferred_element_type=jnp.float32) * out_scale).astype(jnp.bfloat16)
        picked = jnp.take(slab_partial, pair_rows, axis=0).astype(jnp.float32)
        chosen = pair_expert == expert
        return (running + jnp.where(chosen[:, None], picked, jnp.zeros_like(picked)), None)
    pair_sums, unused = lax.scan(add_slab, jnp.zeros((blocks * pair_count, D), jnp.float32), jnp.arange(SLABS, dtype=jnp.int32))
    weighted = pair_sums * next_gates.reshape(-1, 1)
    layer_output = lax.optimization_barrier(jnp.sum(weighted.reshape(-1, TOPK, D), axis=1)).astype(jnp.bfloat16)
    return (layer_output, moved_weights, moved_first, moved_second)
```

```python
import jax
import jax.numpy as jnp
from jax import lax
from jax.sharding import Mesh
from jax.sharding import PartitionSpec as P

D = 2048
HID = 1152
EXPERTS = 4
CAP = 40
SLOTS = EXPERTS * CAP
DP = ("x", "z")
EXPERT = ("y", "core")
ALL = DP + EXPERT
FIRST = 640


beta_one = 0.9
beta_two = 0.95
learn_rate = 0.2
decay_rate = 0.1
adam_step = 10.0
adam_eps = 1e-08


def around(axis, by):
    size = lax.axis_size(axis)
    return [(k, (k + by) % size) for k in range(size)]


def pass_on(value, axis, by):
    return lax.ppermute(value, axis, around(axis, by))


def exchange(value, axis):
    return lax.all_to_all(value, axis, split_axis=0, concat_axis=0, tiled=True)


def slot_of(routes):
    ids = routes.reshape(-1)
    one_hot = ids[:, None] == jnp.arange(EXPERTS, dtype=jnp.int32)[None, :]
    count = ids.shape[0]
    before = lax.broadcasted_iota(jnp.int32, (count, count), 1) < lax.broadcasted_iota(
        jnp.int32, (count, count), 0
    )
    earlier = jnp.dot(
        before.astype(jnp.bfloat16),
        one_hot.astype(jnp.bfloat16),
        preferred_element_type=jnp.float32,
    )
    slots = jnp.sum(jnp.where(one_hot, earlier, 0.0), axis=1).astype(jnp.int32)
    return ids * CAP + slots


def to_slots(targets, payload):
    rows = lax.broadcasted_iota(jnp.int32, (SLOTS, targets.shape[0]), 0)
    selector = (rows == targets[None, :]).astype(jnp.bfloat16)
    filled = jnp.dot(selector, payload, preferred_element_type=jnp.float32)
    return filled.astype(jnp.bfloat16).reshape(EXPERTS, CAP, payload.shape[1])


def after(value, other):
    one = other[(0,) * other.ndim]
    return value + (one != one).astype(value.dtype)


def both_cores(rows):
    return jnp.concatenate([rows, pass_on(rows, "core", 1)], axis=0)


def to_chips(slots):
    chips = lax.axis_size("y")
    return exchange(jnp.repeat(slots, chips // EXPERTS, axis=0), "y")


def chunk_of(parts, offset):
    return lax.dynamic_index_in_dim(
        parts, lax.rem(lax.axis_index("x") + offset, 4), 0, keepdims=False
    )


def f32(value):
    return value.astype(jnp.float32)


def b16(value):
    return value.astype(jnp.bfloat16)


def sum_along_x(parts):
    far = chunk_of(parts, 2)
    half = far.shape[0] // 2
    top = pass_on(far[:half], "x", 1)
    bottom = pass_on(far[half:], "x", -1)
    after, before = chunk_of(parts, 1), chunk_of(parts, 3)
    after = jnp.concatenate([b16(f32(after[:half]) + f32(top)), after[half:]], axis=0)
    before = jnp.concatenate([before[:half], b16(f32(before[half:]) + f32(bottom))], axis=0)
    from_left = pass_on(after, "x", 1)
    from_right = pass_on(before, "x", -1)
    return f32(chunk_of(parts, 0)) + f32(from_left) + f32(from_right)


def sum_small_along_x(parts):
    total = f32(chunk_of(parts, 0))
    for by in (1, 2, 3):
        total = total + f32(pass_on(chunk_of(parts, by), "x", by))
    return total


def in_x_order(found):
    me = lax.axis_index("x")
    out = jnp.zeros((4,) + found[0].shape, found[0].dtype)
    for k, value in enumerate(found):
        out = lax.dynamic_update_index_in_dim(out, value, lax.rem(me + k, 4), 0)
    return out


def gather_along_x(value):
    half = value.shape[0] // 2
    left = pass_on(value, "x", 1)
    right = pass_on(value, "x", -1)
    top = pass_on(left[:half], "x", 1)
    bottom = pass_on(right[half:], "x", -1)
    return in_x_order([value, right, jnp.concatenate([top, bottom], axis=0), left])


def gather_small_along_x(value):
    return in_x_order([value] + [pass_on(value, "x", -by) for by in (1, 2, 3)])


def gather_along_z(value):
    size = lax.axis_size("z")
    return exchange(jnp.broadcast_to(value[None], (size,) + value.shape), "z")


def sum_along_z(value):
    got = exchange(value, "z")
    return jnp.sum(f32(got), axis=0)


def own_rows(first, second):
    size_x, size_z = lax.axis_size("x"), lax.axis_size("z")
    rows = first.shape[0] // (size_x * size_z)
    second = second.reshape(size_x, size_z, rows, -1).swapaxes(0, 1)
    half_second = b16(sum_along_z(second))
    half_first = b16(sum_along_x(first.reshape(size_x, size_z * rows, -1)))
    own_second = sum_small_along_x(half_second)
    own_first = sum_along_z(half_first.reshape(size_z, rows, -1))
    return jnp.concatenate([own_first, own_second], axis=1)


def all_rows(value):
    first, second = value[:, :FIRST], value[:, FIRST:]
    wide_first = gather_along_z(first)
    wide_second = gather_small_along_x(second)
    all_second = gather_along_z(wide_second).swapaxes(0, 1)
    all_first = gather_along_x(wide_first.reshape(-1, wide_first.shape[-1]))
    return (
        all_first.reshape(-1, first.shape[1]),
        all_second.reshape(-1, second.shape[1]),
    )


def whole_step(
    step_inputs,
    step_cotangent,
    step_routes,
    step_gates,
    next_inputs,
    next_routes,
    next_gates,
    master_weights,
    first_moment,
    second_moment,
    owner_plan,
):
    groups = lax.axis_size(EXPERT)
    width = master_weights.shape[2] // 3
    in_scale = D ** (-0.5)
    out_scale = HID ** (-0.5)
    old_weights = master_weights[0]
    step_targets = slot_of(step_routes)
    scaled = b16(f32(step_cotangent) * step_gates)
    sent_inputs = to_slots(step_targets, step_inputs)
    parts = lax.all_gather(b16(old_weights), "x", axis=0)
    parts = lax.all_gather(parts, "z", axis=0)
    weights = parts.swapaxes(0, 1).reshape(D, 3 * width)
    got_inputs = to_chips(sent_inputs)
    got_scaled = to_chips(to_slots(step_targets, scaled))
    flat_inputs = both_cores(got_inputs).reshape(-1, D)
    flat_scaled = both_cores(got_scaled).reshape(-1, D)

    def times(rows, block):
        return jnp.dot(rows, block, preferred_element_type=jnp.float32)

    gate_pre = times(flat_inputs, weights[:, :width]) * in_scale
    up_pre = times(flat_inputs, weights[:, width : 2 * width]) * in_scale
    down_back = times(flat_scaled, weights[:, 2 * width :]) * out_scale
    sigmoid_gate = jax.nn.sigmoid(gate_pre)
    silu_gate = gate_pre * sigmoid_gate
    activation = b16(silu_gate * up_pre)
    gate_grad = b16(down_back * up_pre * sigmoid_gate * (1.0 + gate_pre * (1.0 - sigmoid_gate)))
    up_grad = b16(down_back * silu_gate)
    contract = (((0,), (0,)), ((), ()))

    def gradient_of(rows, grads, scale):
        return b16(
            lax.dot_general(rows, grads, contract, preferred_element_type=jnp.float32) * scale
        )

    gate_part = gradient_of(flat_inputs, gate_grad, in_scale)
    up_part = gradient_of(flat_inputs, up_grad, in_scale)
    down_part = gradient_of(flat_scaled, activation, out_scale)
    cut = FIRST - 2 * width
    gradient = own_rows(
        jnp.concatenate([gate_part, up_part, down_part[:, :cut]], axis=1), down_part[:, cut:]
    )
    first_new = beta_one * first_moment[0] + (1.0 - beta_one) * gradient
    second_new = beta_two * second_moment[0] + (1.0 - beta_two) * gradient * gradient
    first_hat = first_new / (1.0 - beta_one**adam_step)
    second_hat = second_new / (1.0 - beta_two**adam_step)
    new_weights = old_weights - learn_rate * (
        first_hat / (jnp.sqrt(second_hat) + adam_eps) + decay_rate * old_weights
    )
    serve_first, serve_second = all_rows(b16(new_weights))

    positions = jnp.arange(groups, dtype=jnp.int32)
    me = lax.axis_index(EXPERT)
    holder = jnp.sum(jnp.where(owner_plan == me, positions, 0))
    stacked = jnp.concatenate([b16(new_weights), b16(first_new), b16(second_new)], axis=0)
    everywhere = lax.all_gather(stacked, EXPERT, axis=0)
    relocated = lax.dynamic_index_in_dim(everywhere, holder, 0, keepdims=False)
    relocated = f32(relocated).reshape(3, 1, new_weights.shape[0], new_weights.shape[1])

    next_targets = slot_of(next_routes)
    next_slots = to_slots(after(next_targets, got_scaled), next_inputs)
    column = lax.all_gather(next_slots, "y", axis=0)
    chips_each = lax.axis_size("y") // EXPERTS
    here = lax.axis_index("y") // chips_each
    own_next = lax.dynamic_index_in_dim(column, here, 1, keepdims=False).reshape(-1, D)
    other_next = pass_on(own_next, "core", 1)
    down = jnp.concatenate([serve_first[:, 2 * width :], serve_second], axis=1)

    def partial_of(rows):
        gate_next = times(rows, serve_first[:, :width]) * in_scale
        up_next = times(rows, serve_first[:, width : 2 * width]) * in_scale
        next_activation = b16(gate_next * jax.nn.sigmoid(gate_next) * up_next)
        return (
            lax.dot_general(
                next_activation, down, (((1,), (1,)), ((), ())), preferred_element_type=jnp.float32
            )
            * out_scale
        )

    met = pass_on(b16(partial_of(other_next)), "core", 1)
    partials = b16(partial_of(own_next) + f32(met))
    returned = exchange(partials, "y")
    chip_rows = returned.shape[0]
    slot = lax.broadcasted_iota(jnp.int32, (next_targets.shape[0], chip_rows), 1)
    expert_slot = (slot // (chips_each * CAP)) * CAP + lax.rem(slot, CAP)
    picks = (next_targets[:, None] == expert_slot).astype(jnp.bfloat16)
    pair_sums = jnp.dot(picks, returned, preferred_element_type=jnp.float32)
    layer_output = b16(pair_sums * next_gates)
    return (layer_output, relocated[0], relocated[1], relocated[2])


def solution(mesh):
    chips = mesh.devices.reshape(4, -1, mesh.shape["expert"] // 2, 2)
    tokens = P(ALL, None)
    slabs = P(EXPERT, DP, None)
    return jax.shard_map(
        whole_step,
        mesh=Mesh(chips, ALL),
        in_specs=(tokens,) * 7 + (slabs,) * 3 + (P(),),
        out_specs=(tokens,) + (slabs,) * 3,
        check_vma=False,
    )
```

```python
import jax
import jax.numpy as jnp
from jax import lax
from jax.experimental import pallas as pl
from jax.experimental.pallas import tpu as pltpu
from jax.sharding import Mesh
from jax.sharding import PartitionSpec as P

D = 2048
HID = 1152
EXPERTS = 4
CAP = 40
SLOTS = EXPERTS * CAP
DP = ("x", "z")
EXPERT = ("y", "core")
ALL = DP + EXPERT
WIDTH = 288
MAIN = 256
TAIL = WIDTH - MAIN
FIRST = 2 * MAIN + 128
IN_SCALE = 2048 ** (-0.5)
OUT_SCALE = HID ** (-0.5)
TEST = False


beta_one = 0.9
beta_two = 0.95
learn_rate = 0.2
decay_rate = 0.1
adam_step = 10.0
adam_eps = 1e-08


def around(axis, by):
    size = lax.axis_size(axis)
    return [(k, (k + by) % size) for k in range(size)]


def pass_on(value, axis, by):
    return lax.ppermute(value, axis, around(axis, by))


def exchange(value, axis):
    return lax.all_to_all(value, axis, split_axis=0, concat_axis=0, tiled=True)


def slot_of(routes):
    ids = routes.reshape(-1)
    one_hot = ids[:, None] == jnp.arange(EXPERTS, dtype=jnp.int32)[None, :]
    count = ids.shape[0]
    before = lax.broadcasted_iota(jnp.int32, (count, count), 1) < lax.broadcasted_iota(
        jnp.int32, (count, count), 0
    )
    earlier = jnp.dot(
        before.astype(jnp.bfloat16),
        one_hot.astype(jnp.bfloat16),
        preferred_element_type=jnp.float32,
    )
    slots = jnp.sum(jnp.where(one_hot, earlier, 0.0), axis=1).astype(jnp.int32)
    return ids * CAP + slots


def to_slots(targets, payload):
    rows = lax.broadcasted_iota(jnp.int32, (SLOTS, targets.shape[0]), 0)
    selector = (rows == targets[None, :]).astype(jnp.bfloat16)
    filled = jnp.dot(selector, payload, preferred_element_type=jnp.float32)
    return filled.astype(jnp.bfloat16).reshape(EXPERTS, CAP, payload.shape[1])


def after(value, other):
    one = other[(0,) * other.ndim]
    return value + (one != one).astype(value.dtype)


def to_chips(slots):
    chips = lax.axis_size("y")
    return exchange(jnp.repeat(slots, chips // EXPERTS, axis=0), "y")


def chunk_of(parts, offset):
    return lax.dynamic_index_in_dim(
        parts, lax.rem(lax.axis_index("x") + offset, 4), 0, keepdims=False
    )


def f32(value):
    return value.astype(jnp.float32)


def b16(value):
    return value.astype(jnp.bfloat16)


def sum_along_x(parts):
    far = chunk_of(parts, 2)
    half = far.shape[0] // 2
    top = pass_on(far[:half], "x", 1)
    bottom = pass_on(far[half:], "x", -1)
    after, before = chunk_of(parts, 1), chunk_of(parts, 3)
    after = jnp.concatenate([b16(f32(after[:half]) + f32(top)), after[half:]], axis=0)
    before = jnp.concatenate([before[:half], b16(f32(before[half:]) + f32(bottom))], axis=0)
    from_left = pass_on(after, "x", 1)
    from_right = pass_on(before, "x", -1)
    return f32(chunk_of(parts, 0)) + f32(from_left) + f32(from_right)


def sum_small_along_x(parts):
    total = f32(chunk_of(parts, 0))
    for by in (1, 2, 3):
        total = total + f32(pass_on(chunk_of(parts, by), "x", by))
    return total


def in_x_order(found):
    me = lax.axis_index("x")
    out = jnp.zeros((4,) + found[0].shape, found[0].dtype)
    for k, value in enumerate(found):
        out = lax.dynamic_update_index_in_dim(out, value, lax.rem(me + k, 4), 0)
    return out


def gather_small_along_x(value):
    return in_x_order([value] + [pass_on(value, "x", -by) for by in (1, 2, 3)])


def gather_along_z(value):
    size = lax.axis_size("z")
    return exchange(jnp.broadcast_to(value[None], (size,) + value.shape), "z")


def sum_along_z(value):
    got = exchange(value, "z")
    return jnp.sum(f32(got), axis=0)


def arranged(value):
    gate, up, down = (value[:, k * WIDTH : (k + 1) * WIDTH] for k in range(3))
    spare = jnp.zeros((value.shape[0], 128 - 3 * TAIL), value.dtype)
    tails = [gate[:, MAIN:], up[:, MAIN:], down[:, MAIN:], spare]
    return jnp.concatenate([gate[:, :MAIN], up[:, :MAIN]] + tails, axis=1), down[:, :MAIN]


def in_place(first, second):
    tails = [first[:, 2 * MAIN + k * TAIL : 2 * MAIN + (k + 1) * TAIL] for k in range(3)]
    mains = [first[:, :MAIN], first[:, MAIN : 2 * MAIN], second]
    return jnp.concatenate([mains[0], tails[0], mains[1], tails[1], mains[2], tails[2]], axis=1)


def own_rows(first, second):
    size_z, rows = second.shape[0], second.shape[2]
    half_second = b16(sum_along_z(second))
    half_first = b16(sum_along_x(first))
    own_second = sum_small_along_x(half_second)
    own_first = sum_along_z(half_first.reshape(size_z, rows, -1))
    return in_place(own_first, own_second)


def all_rows(value):
    first, second = arranged(value)
    wide_first = gather_along_z(first)
    wide_second = gather_small_along_x(second)
    all_second = gather_along_z(wide_second)
    return found_along_x(wide_first.reshape(-1, wide_first.shape[-1])), all_second


def found_along_x(value):
    half = value.shape[0] // 2
    left = pass_on(value, "x", 1)
    right = pass_on(value, "x", -1)
    top = pass_on(left[:half], "x", 1)
    bottom = pass_on(right[half:], "x", -1)
    return value, right, top, bottom, left


def dot(a, b, dims=((1,), (0,))):
    return lax.dot_general(a, b, (dims, ((), ())), preferred_element_type=jnp.float32)


def lanes(shape):
    return lax.broadcasted_iota(jnp.int32, shape, 1)


def back_terms(gate, up, down_back):
    sigmoid_gate = jax.nn.sigmoid(gate)
    silu_gate = gate * sigmoid_gate
    return (
        silu_gate * up,
        down_back * up * sigmoid_gate * (1.0 + gate * (1.0 - sigmoid_gate)),
        down_back * silu_gate,
    )


def step_body(own_in, other_in, own_sc, other_sc, w, out_a, out_b, wn, pre, dn, g_in, g_sc):
    size_z, size_x, rows = w.shape[:3]
    wide = size_z * rows
    count = own_in.shape[0]
    for k in range(size_x):
        wn[k * wide : (k + 1) * wide, :] = w[:, k].reshape(wide, w.shape[3])
    for half, (taken, scaled) in enumerate(((own_in, own_sc), (other_in, other_sc))):
        span = slice(half * count, (half + 1) * count)
        pre[span, :] = dot(taken[...], wn[:, :FIRST]) * IN_SCALE
        dn[span, :] = dot(scaled[...], wn[:, 2 * MAIN :]) * OUT_SCALE

    def chunk(i, carry):
        at = pl.ds(pl.multiple_of(i * 64, 64), 64)
        act, gate_grad, up_grad = back_terms(
            pre[at, :MAIN], pre[at, MAIN : 2 * MAIN], dn[at, 128:]
        )
        tail, down_tail = pre[at, 2 * MAIN :], dn[at, :128]
        lane = lanes(tail.shape)
        act_t, gate_t, up_t = back_terms(
            tail, pltpu.roll(tail, 128 - TAIL, 1), pltpu.roll(down_tail, 128 - 2 * TAIL, 1)
        )
        tail_in = jnp.where(
            lane < TAIL, gate_t, jnp.where(lane < 2 * TAIL, pltpu.roll(up_t, TAIL, 1), 0.0)
        )
        here = (lane >= 2 * TAIL) & (lane < 3 * TAIL)
        tail_sc = jnp.where(here, pltpu.roll(act_t, 2 * TAIL, 1), 0.0)
        g_in[at, :MAIN] = b16(gate_grad)
        g_in[at, MAIN : 2 * MAIN] = b16(up_grad)
        g_in[at, 2 * MAIN :] = b16(tail_in)
        g_sc[at, :128] = b16(tail_sc)
        g_sc[at, 128:] = b16(act)
        return carry

    lax.fori_loop(0, 2 * count // 64, chunk, 0)
    over_rows = ((0,), (0,))
    for k in range(size_x):
        cols = slice(k * wide, (k + 1) * wide)
        a = dot(own_in[:, cols], g_in[:count, :], over_rows)
        a = (a + dot(other_in[:, cols], g_in[count:, :], over_rows)) * IN_SCALE
        b = dot(own_sc[:, cols], g_sc[:count, :], over_rows)
        b = (b + dot(other_sc[:, cols], g_sc[count:, :], over_rows)) * OUT_SCALE
        out_a[k, :, : 2 * MAIN] = b16(a[:, : 2 * MAIN])
        out_a[k, :, 2 * MAIN :] = b16(a[:, 2 * MAIN :] + b[:, :128])
        out_b[:, k] = b16(b[:, 128:]).reshape(size_z, rows, MAIN)


def step_gradients(own_in, other_in, own_sc, other_sc, w):
    size_z, size_x, rows, columns = w.shape
    count = own_in.shape[0]
    return pl.pallas_call(
        step_body,
        out_shape=(
            jax.ShapeDtypeStruct((size_x, size_z * rows, FIRST), jnp.bfloat16),
            jax.ShapeDtypeStruct((size_z, size_x, rows, MAIN), jnp.bfloat16),
        ),
        scratch_shapes=[
            pltpu.VMEM((D, columns), jnp.bfloat16),
            pltpu.VMEM((2 * count, FIRST), jnp.float32),
            pltpu.VMEM((2 * count, 128 + MAIN), jnp.float32),
            pltpu.VMEM((2 * count, FIRST), jnp.bfloat16),
            pltpu.VMEM((2 * count, 128 + MAIN), jnp.bfloat16),
        ],
        interpret=TEST,
        name="step_gradients",
    )(own_in, other_in, own_sc, other_sc, w)


def serve_body(me, taken, own, right, top, bottom, left, second, out, wn, pre, act):
    size_z, size_x, rows = second.shape[:3]
    wide = size_z * rows
    half = wide // 2

    def start_of(offset):
        return pl.multiple_of(lax.rem(me[0] + offset, size_x) * wide, wide)

    wn[pl.ds(start_of(0), wide), :] = own[...]
    wn[pl.ds(start_of(1), wide), :] = right[...]
    wn[pl.ds(start_of(2), half), :] = top[...]
    wn[pl.ds(pl.multiple_of(start_of(2) + half, half), half), :] = bottom[...]
    wn[pl.ds(start_of(3), wide), :] = left[...]
    pre[...] = dot(taken[...], wn[...]) * IN_SCALE

    def chunk(i, carry):
        at = pl.ds(pl.multiple_of(i * 64, 64), 64)
        gate, up = pre[at, :MAIN], pre[at, MAIN : 2 * MAIN]
        tail = pre[at, 2 * MAIN :]
        lane = lanes(tail.shape)
        act_t = tail * jax.nn.sigmoid(tail) * pltpu.roll(tail, 128 - TAIL, 1)
        here = (lane >= 2 * TAIL) & (lane < 3 * TAIL)
        act[at, :128] = b16(jnp.where(here, pltpu.roll(act_t, 2 * TAIL, 1), 0.0))
        act[at, 128:] = b16(gate * jax.nn.sigmoid(gate) * up)
        return carry

    lax.fori_loop(0, taken.shape[0] // 64, chunk, 0)
    for k in range(size_x):
        cols = slice(k * wide, (k + 1) * wide)
        total = dot(act[:, :128], wn[cols, 2 * MAIN :], ((1,), (1,)))
        total = total + dot(act[:, 128:], second[:, k].reshape(wide, MAIN), ((1,), (1,)))
        out[:, cols] = b16(total * OUT_SCALE)


def serve(taken, pieces, second):
    me = lax.axis_index("x").astype(jnp.int32).reshape(1)
    return pl.pallas_call(
        serve_body,
        out_shape=jax.ShapeDtypeStruct(taken.shape, jnp.bfloat16),
        in_specs=[pl.BlockSpec(memory_space=pltpu.SMEM)]
        + [pl.BlockSpec(memory_space=pltpu.VMEM)] * 7,
        scratch_shapes=[
            pltpu.VMEM((D, FIRST), jnp.bfloat16),
            pltpu.VMEM((taken.shape[0], FIRST), jnp.float32),
            pltpu.VMEM((taken.shape[0], 128 + MAIN), jnp.bfloat16),
        ],
        interpret=TEST,
        name="serve",
    )(me, taken, *pieces, second)


def whole_step(
    step_inputs,
    step_cotangent,
    step_routes,
    step_gates,
    next_inputs,
    next_routes,
    next_gates,
    master_weights,
    first_moment,
    second_moment,
    owner_plan,
):
    groups = lax.axis_size(EXPERT)
    old_weights = master_weights[0]
    step_targets = slot_of(step_routes)
    scaled = b16(f32(step_cotangent) * step_gates)
    sent_inputs = to_slots(step_targets, step_inputs)
    parts = lax.all_gather(
        jnp.concatenate(arranged(b16(old_weights)), axis=1), "x", axis=0
    )
    weights = lax.all_gather(parts, "z", axis=0)
    got_inputs = to_chips(sent_inputs)
    got_scaled = to_chips(to_slots(step_targets, scaled))
    other_inputs = pass_on(got_inputs, "core", 1)
    other_scaled = pass_on(got_scaled, "core", 1)
    rows_in_scaled = [
        rows.reshape(-1, D) for rows in (got_inputs, other_inputs, got_scaled, other_scaled)
    ]
    gradient = own_rows(*step_gradients(*rows_in_scaled, weights))
    first_new = beta_one * first_moment[0] + (1.0 - beta_one) * gradient
    second_new = beta_two * second_moment[0] + (1.0 - beta_two) * gradient * gradient
    first_hat = first_new / (1.0 - beta_one**adam_step)
    second_hat = second_new / (1.0 - beta_two**adam_step)
    new_weights = old_weights - learn_rate * (
        first_hat / (jnp.sqrt(second_hat) + adam_eps) + decay_rate * old_weights
    )
    pieces, second = all_rows(b16(new_weights))

    positions = jnp.arange(groups, dtype=jnp.int32)
    me = lax.axis_index(EXPERT)
    holder = jnp.sum(jnp.where(owner_plan == me, positions, 0))
    stacked = jnp.concatenate([b16(new_weights), b16(first_new), b16(second_new)], axis=0)
    everywhere = lax.all_gather(stacked, EXPERT, axis=0)
    relocated = lax.dynamic_index_in_dim(everywhere, holder, 0, keepdims=False)
    relocated = f32(relocated).reshape(3, 1, new_weights.shape[0], new_weights.shape[1])

    next_targets = slot_of(next_routes)
    next_slots = to_slots(after(next_targets, other_inputs), next_inputs)
    column = lax.all_gather(next_slots, "y", axis=0)
    chips_each = lax.axis_size("y") // EXPERTS
    here = lax.axis_index("y") // chips_each
    own_next = lax.dynamic_index_in_dim(column, here, 1, keepdims=False).reshape(-1, D)
    other_next = pass_on(own_next, "core", 1)
    met = pass_on(serve(other_next, pieces, second), "core", 1)
    partials = b16(f32(serve(own_next, pieces, second)) + f32(met))
    partials = partials.reshape(-1, CAP, D)
    returned = exchange(partials, "y")
    returned = returned.reshape(-1, D)
    chip_rows = returned.shape[0]
    slot = lax.broadcasted_iota(jnp.int32, (next_targets.shape[0], chip_rows), 1)
    expert_slot = (slot // (chips_each * CAP)) * CAP + lax.rem(slot, CAP)
    picks = (next_targets[:, None] == expert_slot).astype(jnp.bfloat16)
    pair_sums = jnp.dot(picks, returned, preferred_element_type=jnp.float32)
    layer_output = b16(pair_sums * next_gates)
    return (layer_output, relocated[0], relocated[1], relocated[2])


def solution(mesh):
    chips = mesh.devices.reshape(4, -1, mesh.shape["expert"] // 2, 2)
    tokens = P(ALL, None)
    slabs = P(EXPERT, DP, None)
    return jax.shard_map(
        whole_step,
        mesh=Mesh(chips, ALL),
        in_specs=(tokens,) * 7 + (slabs,) * 3 + (P(),),
        out_specs=(tokens,) + (slabs,) * 3,
        check_vma=False,
    )
```

```python
import jax
import jax.numpy as jnp
from jax import lax
from jax.experimental import pallas as pl
from jax.experimental.pallas import tpu as pltpu
from jax.sharding import Mesh
from jax.sharding import PartitionSpec as P

D = 2048
HID = 1152
EXPERTS = 4
CAP = 40
SLOTS = EXPERTS * CAP
DP = ("x", "z")
EXPERT = ("y", "core")
ALL = DP + EXPERT
WIDTH = 288
MAIN = 256
TAIL = WIDTH - MAIN
LEAD = 2 * MAIN
SIDE = 128 + MAIN
COLS = LEAD + SIDE
IN_SCALE = 2048 ** (-0.5)
OUT_SCALE = HID ** (-0.5)
TEST = False


beta_one = 0.9
beta_two = 0.95
learn_rate = 0.2
decay_rate = 0.1
adam_step = 10.0
adam_eps = 1e-08


def pass_on(value, axis, by):
    size = lax.axis_size(axis)
    return lax.ppermute(value, axis, [(k, (k + by) % size) for k in range(size)])


def exchange(value, axis):
    return lax.all_to_all(value, axis, split_axis=0, concat_axis=0, tiled=True)


def f32(value):
    return value.astype(jnp.float32)


def b16(value):
    return value.astype(jnp.bfloat16)


def slot_of(routes):
    ids = routes.reshape(-1)
    one_hot = ids[:, None] == jnp.arange(EXPERTS, dtype=jnp.int32)[None, :]
    count = ids.shape[0]
    before = lax.broadcasted_iota(jnp.int32, (count, count), 1) < lax.broadcasted_iota(
        jnp.int32, (count, count), 0
    )
    earlier = jnp.dot(
        before.astype(jnp.bfloat16),
        one_hot.astype(jnp.bfloat16),
        preferred_element_type=jnp.float32,
    )
    slots = jnp.sum(jnp.where(one_hot, earlier, 0.0), axis=1).astype(jnp.int32)
    return ids * CAP + slots


def to_slots(targets, payload):
    rows = lax.broadcasted_iota(jnp.int32, (SLOTS, targets.shape[0]), 0)
    selector = (rows == targets[None, :]).astype(jnp.bfloat16)
    filled = jnp.dot(selector, payload, preferred_element_type=jnp.float32)
    return filled.astype(jnp.bfloat16).reshape(EXPERTS, CAP, payload.shape[1])


def to_chips(slots):
    chips = lax.axis_size("y")
    return exchange(jnp.repeat(slots, chips // EXPERTS, axis=0), "y").reshape(-1, D)


def arranged(value):
    gate, up, down = (value[:, k * WIDTH : (k + 1) * WIDTH] for k in range(3))
    spare = jnp.zeros((value.shape[0], 128 - 3 * TAIL), value.dtype)
    tails = [gate[:, MAIN:], up[:, MAIN:], down[:, MAIN:], spare]
    return jnp.concatenate([gate[:, :MAIN], up[:, :MAIN]] + tails + [down[:, :MAIN]], axis=1)


def in_place(value):
    parts = []
    for k, start in enumerate((0, MAIN, LEAD + 128)):
        at = LEAD + k * TAIL
        parts += [value[:, start : start + MAIN], value[:, at : at + TAIL]]
    return jnp.concatenate(parts, axis=1)


def found_along_x(value):
    half = value.shape[0] // 2
    left = pass_on(value, "x", 1)
    right = pass_on(value, "x", -1)
    top = pass_on(left[:half], "x", 1)
    bottom = pass_on(right[half:], "x", -1)
    return value, right, top, bottom, left


def found_along_z(value):
    size = lax.axis_size("z")
    me = lax.axis_index("z")
    out = jnp.zeros((size,) + value.shape, value.dtype)
    out = lax.dynamic_update_index_in_dim(out, value, me, 0)
    for by in range(1, size):
        got = pass_on(value, "z", -by)
        out = lax.dynamic_update_index_in_dim(out, got, lax.rem(me + by, size), 0)
    return out.reshape(-1, value.shape[1])


def own_rows(right, left, near, own):
    half = own.shape[0] // 2
    from_left = pass_on(right, "x", 1)
    from_right = pass_on(left, "x", -1)
    top = pass_on(b16(f32(near[0]) + f32(from_left[:half])), "x", 1)
    bottom = pass_on(b16(f32(near[1]) + f32(from_right[:half])), "x", -1)
    first = f32(own[:half]) + f32(from_right[half:]) + f32(top)
    second = f32(own[half:]) + f32(from_left[half:]) + f32(bottom)
    summed = b16(jnp.concatenate([first, second], axis=0))
    parts = exchange(summed.reshape(lax.axis_size("z"), -1, COLS), "z")
    return in_place(jnp.sum(f32(parts), axis=0))


def all_rows(value):
    size = lax.axis_size("z")
    wide = exchange(jnp.broadcast_to(value[None], (size,) + value.shape), "z")
    return found_along_x(wide.reshape(-1, COLS))


def dot(a, b, dims=((1,), (0,))):
    return lax.dot_general(a, b, (dims, ((), ())), preferred_element_type=jnp.float32)


def lanes(shape):
    return lax.broadcasted_iota(jnp.int32, shape, 1)


def start_of(me, offset, wide):
    return pl.multiple_of(lax.rem(me + offset, 4) * wide, wide)


def in_row_order(me, pieces, wn, columns):
    own, right, top, bottom, left = pieces
    wide = own.shape[0]
    half = wide // 2
    wn[pl.ds(start_of(me, 0, wide), wide), :] = own[:, columns]
    wn[pl.ds(start_of(me, 1, wide), wide), :] = right[:, columns]
    far = start_of(me, 2, wide)
    wn[pl.ds(far, half), :] = top[:, columns]
    wn[pl.ds(pl.multiple_of(far + half, half), half), :] = bottom[:, columns]
    wn[pl.ds(start_of(me, 3, wide), wide), :] = left[:, columns]


def pre_body(me, own_in, other_in, own, right, top, bottom, left, act, silu, slope, wn, pre):
    in_row_order(me[0], (own, right, top, bottom, left), wn, slice(0, LEAD + 128))
    count = own_in.shape[0]
    for half, taken in enumerate((own_in, other_in)):
        pre[half * count : (half + 1) * count, :] = dot(taken[...], wn[...]) * IN_SCALE

    def chunk(i, carry):
        at = pl.ds(pl.multiple_of(i * 64, 64), 64)
        tail = pre[at, LEAD:]
        pairs = (
            (tail, pltpu.roll(tail, 128 - TAIL, 1), slice(0, 128)),
            (pre[at, :MAIN], pre[at, MAIN:LEAD], slice(128, SIDE)),
        )
        for gate, up, cols in pairs:
            sigmoid_gate = jax.nn.sigmoid(gate)
            silu_gate = gate * sigmoid_gate
            product = silu_gate * up
            if cols.start == 0:
                lane = lanes(tail.shape)
                here = (lane >= 2 * TAIL) & (lane < 3 * TAIL)
                product = jnp.where(here, pltpu.roll(product, 2 * TAIL, 1), 0.0)
            act[at, cols] = b16(product)
            silu[at, cols] = silu_gate
            slope[at, cols] = up * sigmoid_gate * (1.0 + gate * (1.0 - sigmoid_gate))
        return carry

    lax.fori_loop(0, 2 * count // 64, chunk, 0)


def step_pre(own_in, other_in, pieces):
    me = lax.axis_index("x").astype(jnp.int32).reshape(1)
    count = 2 * own_in.shape[0]
    return pl.pallas_call(
        pre_body,
        out_shape=(
            jax.ShapeDtypeStruct((count, SIDE), jnp.bfloat16),
            jax.ShapeDtypeStruct((count, SIDE), jnp.float32),
            jax.ShapeDtypeStruct((count, SIDE), jnp.float32),
        ),
        in_specs=[pl.BlockSpec(memory_space=pltpu.SMEM)]
        + [pl.BlockSpec(memory_space=pltpu.VMEM)] * 7,
        scratch_shapes=[
            pltpu.VMEM((D, LEAD + 128), jnp.bfloat16),
            pltpu.VMEM((count, LEAD + 128), jnp.float32),
        ],
        interpret=TEST,
        name="step_pre",
    )(me, own_in, other_in, *pieces)


def terms_body(
    me, own_in, other_in, own_sc, other_sc, act, silu, slope, own, right, top, bottom, left,
    to_right, to_left, near, mine, wn, dn, g_in,
):
    in_row_order(me[0], (own, right, top, bottom, left), wn, slice(LEAD, COLS))
    count = own_in.shape[0]
    for half, scaled in enumerate((own_sc, other_sc)):
        dn[half * count : (half + 1) * count, :] = dot(scaled[...], wn[...]) * OUT_SCALE

    def chunk(i, carry):
        at = pl.ds(pl.multiple_of(i * 64, 64), 64)
        down_back = dn[at, 128:]
        g_in[at, :MAIN] = b16(down_back * slope[at, 128:])
        g_in[at, MAIN:LEAD] = b16(down_back * silu[at, 128:])
        down_tail = pltpu.roll(dn[at, :128], 128 - 2 * TAIL, 1)
        gate_t, up_t = down_tail * slope[at, :128], down_tail * silu[at, :128]
        lane = lanes(gate_t.shape)
        up_t = jnp.where(lane < 2 * TAIL, pltpu.roll(up_t, TAIL, 1), 0.0)
        g_in[at, LEAD:] = b16(jnp.where(lane < TAIL, gate_t, up_t))
        return carry

    lax.fori_loop(0, 2 * count // 64, chunk, 0)
    over_rows = ((0,), (0,))
    wide = own.shape[0]
    half = wide // 2
    for k in range(4):
        cols = pl.ds(start_of(me[0], k, wide), wide)
        a = dot(own_in[:, cols], g_in[:count, :], over_rows)
        a = (a + dot(other_in[:, cols], g_in[count:, :], over_rows)) * IN_SCALE
        b = dot(own_sc[:, cols], act[:count, :], over_rows)
        b = (b + dot(other_sc[:, cols], act[count:, :], over_rows)) * OUT_SCALE
        parts = (
            (slice(0, LEAD), b16(a[:, :LEAD])),
            (slice(LEAD, LEAD + 128), b16(a[:, LEAD:] + b[:, :128])),
            (slice(LEAD + 128, COLS), b16(b[:, 128:])),
        )
        for at, value in parts:
            if k == 0:
                mine[:, at] = value
            elif k == 1:
                near[0, :, at] = value[:half]
                to_right[half:, at] = value[half:]
            elif k == 2:
                to_right[:half, at] = value[:half]
                to_left[:half, at] = value[half:]
            else:
                to_left[half:, at] = value[:half]
                near[1, :, at] = value[half:]


def step_terms(rows, made, pieces):
    me = lax.axis_index("x").astype(jnp.int32).reshape(1)
    count = 2 * rows[0].shape[0]
    wide = pieces[0].shape[0]
    chunk = jax.ShapeDtypeStruct((wide, COLS), jnp.bfloat16)
    return pl.pallas_call(
        terms_body,
        out_shape=(
            chunk,
            chunk,
            jax.ShapeDtypeStruct((2, wide // 2, COLS), jnp.bfloat16),
            chunk,
        ),
        in_specs=[pl.BlockSpec(memory_space=pltpu.SMEM)]
        + [pl.BlockSpec(memory_space=pltpu.VMEM)] * 12,
        scratch_shapes=[
            pltpu.VMEM((D, SIDE), jnp.bfloat16),
            pltpu.VMEM((count, SIDE), jnp.float32),
            pltpu.VMEM((count, LEAD + 128), jnp.bfloat16),
        ],
        interpret=TEST,
        name="step_terms",
    )(me, *rows, *made, *pieces)


def serve_body(me, taken, own, right, top, bottom, left, out, wn, pre, act):
    in_row_order(me[0], (own, right, top, bottom, left), wn, slice(0, COLS))
    pre[...] = dot(taken[...], wn[:, : LEAD + 128]) * IN_SCALE

    def chunk(i, carry):
        at = pl.ds(pl.multiple_of(i * 64, 64), 64)
        gate, up = pre[at, :MAIN], pre[at, MAIN:LEAD]
        tail = pre[at, LEAD:]
        lane = lanes(tail.shape)
        act_t = tail * jax.nn.sigmoid(tail) * pltpu.roll(tail, 128 - TAIL, 1)
        here = (lane >= 2 * TAIL) & (lane < 3 * TAIL)
        act[at, :128] = b16(jnp.where(here, pltpu.roll(act_t, 2 * TAIL, 1), 0.0))
        act[at, 128:] = b16(gate * jax.nn.sigmoid(gate) * up)
        return carry

    lax.fori_loop(0, taken.shape[0] // 64, chunk, 0)
    wide = own.shape[0]
    for k in range(4):
        cols = slice(k * wide, (k + 1) * wide)
        total = dot(act[...], wn[cols, LEAD:], ((1,), (1,)))
        out[:, cols] = b16(total * OUT_SCALE)


def serve(taken, pieces):
    me = lax.axis_index("x").astype(jnp.int32).reshape(1)
    return pl.pallas_call(
        serve_body,
        out_shape=jax.ShapeDtypeStruct(taken.shape, jnp.bfloat16),
        in_specs=[pl.BlockSpec(memory_space=pltpu.SMEM)]
        + [pl.BlockSpec(memory_space=pltpu.VMEM)] * 6,
        scratch_shapes=[
            pltpu.VMEM((D, COLS), jnp.bfloat16),
            pltpu.VMEM((taken.shape[0], LEAD + 128), jnp.float32),
            pltpu.VMEM((taken.shape[0], SIDE), jnp.bfloat16),
        ],
        interpret=TEST,
        name="serve",
    )(me, taken, *pieces)


def migrated(stacked, owner_plan):
    groups = lax.axis_size(EXPERT)
    positions = jnp.arange(groups, dtype=jnp.int32)
    goes = owner_plan[None, :] == positions[:, None]
    holder = jnp.sum(jnp.where(goes, positions[None, :], 0), axis=1)
    pieces = stacked.reshape(groups, -1, stacked.shape[1])
    spread = exchange(pieces, EXPERT)
    ordered = jnp.take(spread, holder, axis=0)
    return exchange(ordered, EXPERT).reshape(stacked.shape)


def whole_step(
    step_inputs,
    step_cotangent,
    step_routes,
    step_gates,
    next_inputs,
    next_routes,
    next_gates,
    master_weights,
    first_moment,
    second_moment,
    owner_plan,
):
    old_weights = master_weights[0]
    step_targets = slot_of(step_routes)
    scaled = b16(f32(step_cotangent) * step_gates)
    old_wide = found_along_z(arranged(b16(old_weights)))
    old_pieces = found_along_x(old_wide)
    own_in = to_chips(to_slots(step_targets, step_inputs))
    own_sc = to_chips(to_slots(step_targets, scaled))
    other_in = pass_on(own_in, "core", 1)
    other_sc = pass_on(own_sc, "core", 1)
    made = step_pre(own_in, other_in, old_pieces)
    gradient = own_rows(*step_terms((own_in, other_in, own_sc, other_sc), made, old_pieces))
    first_new = beta_one * first_moment[0] + (1.0 - beta_one) * gradient
    second_new = beta_two * second_moment[0] + (1.0 - beta_two) * gradient * gradient
    first_hat = first_new / (1.0 - beta_one**adam_step)
    second_hat = second_new / (1.0 - beta_two**adam_step)
    new_weights = old_weights - learn_rate * (
        first_hat / (jnp.sqrt(second_hat) + adam_eps) + decay_rate * old_weights
    )
    pieces = all_rows(arranged(b16(new_weights)))
    stacked = jnp.concatenate([b16(new_weights), b16(first_new), b16(second_new)], axis=0)
    moved = f32(migrated(stacked, owner_plan)).reshape((3, 1) + old_weights.shape)

    next_targets = slot_of(next_routes)
    own_next = to_chips(to_slots(next_targets, next_inputs))
    other_next = pass_on(own_next, "core", 1)
    met = serve(other_next, pieces)
    met = pass_on(met, "core", 1)
    partials = b16(f32(serve(own_next, pieces)) + f32(met))
    returned = exchange(partials.reshape(-1, CAP, D), "y").reshape(-1, D)
    chips_each = lax.axis_size("y") // EXPERTS
    slot = lax.broadcasted_iota(jnp.int32, (next_targets.shape[0], returned.shape[0]), 1)
    expert_slot = (slot // (chips_each * CAP)) * CAP + lax.rem(slot, CAP)
    picks = (next_targets[:, None] == expert_slot).astype(jnp.bfloat16)
    pair_sums = jnp.dot(picks, returned, preferred_element_type=jnp.float32)
    layer_output = b16(pair_sums * next_gates)
    return (layer_output, moved[0], moved[1], moved[2])


def solution(mesh):
    chips = mesh.devices.reshape(4, -1, mesh.shape["expert"] // 2, 2)
    tokens = P(ALL, None)
    slabs = P(EXPERT, DP, None)
    return jax.shard_map(
        whole_step,
        mesh=Mesh(chips, ALL),
        in_specs=(tokens,) * 7 + (slabs,) * 3 + (P(),),
        out_specs=(tokens,) + (slabs,) * 3,
        check_vma=False,
    )
```

```python
import jax
import jax.numpy as jnp
from jax import lax
from jax.experimental import pallas as pl
from jax.experimental.pallas import tpu as pltpu
from jax.sharding import Mesh
from jax.sharding import PartitionSpec as P

D = 2048
HID = 1152
EXPERTS = 4
CAP = 40
SLOTS = EXPERTS * CAP
DP = ("x", "z")
EXPERT = ("y", "core")
ALL = DP + EXPERT
WIDTH = 288
MAIN = 256
TAIL = WIDTH - MAIN
LEAD = 2 * MAIN
SIDE = 128 + MAIN
COLS = LEAD + SIDE
IN_SCALE = 2048 ** (-0.5)
OUT_SCALE = HID ** (-0.5)
TEST = False


beta_one = 0.9
beta_two = 0.95
learn_rate = 0.2
decay_rate = 0.1
adam_step = 10.0
adam_eps = 1e-08


def pass_on(value, axis, by):
    size = lax.axis_size(axis)
    return lax.ppermute(value, axis, [(k, (k + by) % size) for k in range(size)])


def exchange(value, axis):
    return lax.all_to_all(value, axis, split_axis=0, concat_axis=0, tiled=True)


def f32(value):
    return value.astype(jnp.float32)


def b16(value):
    return value.astype(jnp.bfloat16)


def slot_of(routes):
    ids = routes.reshape(-1)
    one_hot = ids[:, None] == jnp.arange(EXPERTS, dtype=jnp.int32)[None, :]
    count = ids.shape[0]
    before = lax.broadcasted_iota(jnp.int32, (count, count), 1) < lax.broadcasted_iota(
        jnp.int32, (count, count), 0
    )
    earlier = jnp.dot(
        before.astype(jnp.bfloat16),
        one_hot.astype(jnp.bfloat16),
        preferred_element_type=jnp.float32,
    )
    slots = jnp.sum(jnp.where(one_hot, earlier, 0.0), axis=1).astype(jnp.int32)
    return ids * CAP + slots


def to_slots(targets, payload):
    rows = lax.broadcasted_iota(jnp.int32, (SLOTS, targets.shape[0]), 0)
    selector = (rows == targets[None, :]).astype(jnp.bfloat16)
    filled = jnp.dot(selector, payload, preferred_element_type=jnp.float32)
    return filled.astype(jnp.bfloat16).reshape(EXPERTS, CAP, payload.shape[1])


def to_pairs(routes, targets, inputs, scaled):
    chips = lax.axis_size("y")
    me = lax.axis_index("y")
    pair, odd = me // 2, lax.rem(me, 2)
    ids = routes.reshape(-1)
    away = lax.rem(ids - pair + EXPERTS, EXPERTS)
    away = jnp.where(odd == 1, lax.rem(EXPERTS - away, EXPERTS), away)
    places = targets - ids * CAP + away * CAP
    blocks = jnp.stack([to_slots(places, inputs), to_slots(places, scaled)], axis=1)

    def hop(value, step):
        ends = [(k, (k + step if k % 2 == 0 else k - step) % chips) for k in range(chips)]
        return lax.ppermute(value, "y", ends)

    met = [blocks[0], hop(blocks[3], -1), hop(blocks[1], 2), hop(blocks[2], -3)]
    met += [hop(block, 1) for block in met]
    met += [pass_on(block, "core", 1) for block in met]
    return [jnp.concatenate([block[k] for block in met], axis=0) for k in range(2)]


def to_chips(slots):
    chips = lax.axis_size("y")
    return exchange(jnp.repeat(slots, chips // EXPERTS, axis=0), "y").reshape(-1, D)


def arranged(value):
    gate, up, down = (value[:, k * WIDTH : (k + 1) * WIDTH] for k in range(3))
    spare = jnp.zeros((value.shape[0], 128 - 3 * TAIL), value.dtype)
    tails = [gate[:, MAIN:], up[:, MAIN:], down[:, MAIN:], spare]
    return jnp.concatenate([gate[:, :MAIN], up[:, :MAIN]] + tails + [down[:, :MAIN]], axis=1)


def in_place(value):
    parts = []
    for k, start in enumerate((0, MAIN, LEAD + 128)):
        at = LEAD + k * TAIL
        parts += [value[:, start : start + MAIN], value[:, at : at + TAIL]]
    return jnp.concatenate(parts, axis=1)


def found_along_x(value):
    half = value.shape[0] // 2
    left = pass_on(value, "x", 1)
    right = pass_on(value, "x", -1)
    top = pass_on(left[:half], "x", 1)
    bottom = pass_on(right[half:], "x", -1)
    return value, right, top, bottom, left


def own_rows(right, left, near, own):
    half = own.shape[0] // 2
    from_left = pass_on(right, "x", 1)
    from_right = pass_on(left, "x", -1)
    top = pass_on(b16(f32(near[0]) + f32(from_left[:half])), "x", 1)
    bottom = pass_on(b16(f32(near[1]) + f32(from_right[:half])), "x", -1)
    first = f32(own[:half]) + f32(from_right[half:]) + f32(top)
    second = f32(own[half:]) + f32(from_left[half:]) + f32(bottom)
    summed = b16(jnp.concatenate([first, second], axis=0))
    parts = exchange(summed.reshape(lax.axis_size("z"), -1, COLS), "z")
    return in_place(jnp.sum(f32(parts), axis=0))


def all_rows(value):
    size = lax.axis_size("z")
    wide = exchange(jnp.broadcast_to(value[None], (size,) + value.shape), "z")
    return found_along_x(wide.reshape(-1, COLS))


def dot(a, b, dims=((1,), (0,))):
    return lax.dot_general(a, b, (dims, ((), ())), preferred_element_type=jnp.float32)


def lanes(shape):
    return lax.broadcasted_iota(jnp.int32, shape, 1)


def start_of(me, offset, wide):
    return pl.multiple_of(lax.rem(me + offset, 4) * wide, wide)


def in_row_order(me, pieces, wn, columns):
    own, right, top, bottom, left = pieces
    wide = own.shape[0]
    half = wide // 2
    wn[pl.ds(start_of(me, 0, wide), wide), :] = own[:, columns]
    wn[pl.ds(start_of(me, 1, wide), wide), :] = right[:, columns]
    far = start_of(me, 2, wide)
    wn[pl.ds(far, half), :] = top[:, columns]
    wn[pl.ds(pl.multiple_of(far + half, half), half), :] = bottom[:, columns]
    wn[pl.ds(start_of(me, 3, wide), wide), :] = left[:, columns]


def back_terms(gate, up, down_back):
    sigmoid_gate = jax.nn.sigmoid(gate)
    silu_gate = gate * sigmoid_gate
    return (
        silu_gate * up,
        down_back * up * sigmoid_gate * (1.0 + gate * (1.0 - sigmoid_gate)),
        down_back * silu_gate,
    )


def terms_body(
    me, taken, scaled, own, right, top, bottom, left,
    to_right, to_left, near, mine, wn, pre, dn, g_in, g_sc,
):
    in_row_order(me[0], (own, right, top, bottom, left), wn, slice(0, COLS))
    count = taken.shape[0]
    pre[...] = dot(taken[...], wn[:, : LEAD + 128]) * IN_SCALE
    dn[...] = dot(scaled[...], wn[:, LEAD:]) * OUT_SCALE

    def chunk(i, carry):
        at = pl.ds(pl.multiple_of(i * 64, 64), 64)
        act, gate_grad, up_grad = back_terms(pre[at, :MAIN], pre[at, MAIN:LEAD], dn[at, 128:])
        tail, down_tail = pre[at, LEAD:], dn[at, :128]
        lane = lanes(tail.shape)
        act_t, gate_t, up_t = back_terms(
            tail, pltpu.roll(tail, 128 - TAIL, 1), pltpu.roll(down_tail, 128 - 2 * TAIL, 1)
        )
        up_t = jnp.where(lane < 2 * TAIL, pltpu.roll(up_t, TAIL, 1), 0.0)
        here = (lane >= 2 * TAIL) & (lane < 3 * TAIL)
        g_in[at, :MAIN] = b16(gate_grad)
        g_in[at, MAIN:LEAD] = b16(up_grad)
        g_in[at, LEAD:] = b16(jnp.where(lane < TAIL, gate_t, up_t))
        g_sc[at, :128] = b16(jnp.where(here, pltpu.roll(act_t, 2 * TAIL, 1), 0.0))
        g_sc[at, 128:] = b16(act)
        return carry

    lax.fori_loop(0, count // 64, chunk, 0)
    over_rows = ((0,), (0,))
    wide = own.shape[0]
    half = wide // 2
    for k in range(4):
        cols = pl.ds(start_of(me[0], k, wide), wide)
        a = dot(taken[:, cols], g_in[...], over_rows) * IN_SCALE
        b = dot(scaled[:, cols], g_sc[...], over_rows) * OUT_SCALE
        parts = (
            (slice(0, LEAD), b16(a[:, :LEAD])),
            (slice(LEAD, LEAD + 128), b16(a[:, LEAD:] + b[:, :128])),
            (slice(LEAD + 128, COLS), b16(b[:, 128:])),
        )
        for at, value in parts:
            if k == 0:
                mine[:, at] = value
            elif k == 1:
                near[0, :, at] = value[:half]
                to_right[half:, at] = value[half:]
            elif k == 2:
                to_right[:half, at] = value[:half]
                to_left[:half, at] = value[half:]
            else:
                to_left[half:, at] = value[:half]
                near[1, :, at] = value[half:]


def step_terms(taken, scaled, pieces):
    me = lax.axis_index("x").astype(jnp.int32).reshape(1)
    count = taken.shape[0]
    wide = pieces[0].shape[0]
    chunk = jax.ShapeDtypeStruct((wide, COLS), jnp.bfloat16)
    return pl.pallas_call(
        terms_body,
        out_shape=(
            chunk,
            chunk,
            jax.ShapeDtypeStruct((2, wide // 2, COLS), jnp.bfloat16),
            chunk,
        ),
        in_specs=[pl.BlockSpec(memory_space=pltpu.SMEM)]
        + [pl.BlockSpec(memory_space=pltpu.VMEM)] * 7,
        scratch_shapes=[
            pltpu.VMEM((D, COLS), jnp.bfloat16),
            pltpu.VMEM((count, LEAD + 128), jnp.float32),
            pltpu.VMEM((count, SIDE), jnp.float32),
            pltpu.VMEM((count, LEAD + 128), jnp.bfloat16),
            pltpu.VMEM((count, SIDE), jnp.bfloat16),
        ],
        interpret=TEST,
        name="step_terms",
    )(me, taken, scaled, *pieces)


def serve_body(me, taken, own, right, top, bottom, left, out, wn, pre, act):
    in_row_order(me[0], (own, right, top, bottom, left), wn, slice(0, COLS))
    pre[...] = dot(taken[...], wn[:, : LEAD + 128]) * IN_SCALE

    def chunk(i, carry):
        at = pl.ds(pl.multiple_of(i * 64, 64), 64)
        gate, up = pre[at, :MAIN], pre[at, MAIN:LEAD]
        tail = pre[at, LEAD:]
        lane = lanes(tail.shape)
        act_t = tail * jax.nn.sigmoid(tail) * pltpu.roll(tail, 128 - TAIL, 1)
        here = (lane >= 2 * TAIL) & (lane < 3 * TAIL)
        act[at, :128] = b16(jnp.where(here, pltpu.roll(act_t, 2 * TAIL, 1), 0.0))
        act[at, 128:] = b16(gate * jax.nn.sigmoid(gate) * up)
        return carry

    lax.fori_loop(0, taken.shape[0] // 64, chunk, 0)
    wide = own.shape[0]
    for k in range(4):
        cols = slice(k * wide, (k + 1) * wide)
        total = dot(act[...], wn[cols, LEAD:], ((1,), (1,)))
        out[:, cols] = b16(total * OUT_SCALE)


def serve(taken, pieces):
    me = lax.axis_index("x").astype(jnp.int32).reshape(1)
    return pl.pallas_call(
        serve_body,
        out_shape=jax.ShapeDtypeStruct(taken.shape, jnp.bfloat16),
        in_specs=[pl.BlockSpec(memory_space=pltpu.SMEM)]
        + [pl.BlockSpec(memory_space=pltpu.VMEM)] * 6,
        scratch_shapes=[
            pltpu.VMEM((D, COLS), jnp.bfloat16),
            pltpu.VMEM((taken.shape[0], LEAD + 128), jnp.float32),
            pltpu.VMEM((taken.shape[0], SIDE), jnp.bfloat16),
        ],
        interpret=TEST,
        name="serve",
    )(me, taken, *pieces)


def migrated(stacked, owner_plan):
    groups = lax.axis_size(EXPERT)
    positions = jnp.arange(groups, dtype=jnp.int32)
    goes = owner_plan[None, :] == positions[:, None]
    holder = jnp.sum(jnp.where(goes, positions[None, :], 0), axis=1)
    pieces = stacked.reshape(groups, -1, stacked.shape[1])
    spread = exchange(pieces, EXPERT)
    ordered = jnp.take(spread, holder, axis=0)
    return exchange(ordered, EXPERT).reshape(stacked.shape)


def whole_step(
    step_inputs,
    step_cotangent,
    step_routes,
    step_gates,
    next_inputs,
    next_routes,
    next_gates,
    master_weights,
    first_moment,
    second_moment,
    owner_plan,
):
    old_weights = master_weights[0]
    step_targets = slot_of(step_routes)
    scaled = b16(f32(step_cotangent) * step_gates)
    old_pieces = all_rows(arranged(b16(old_weights)))
    taken, taken_scaled = to_pairs(step_routes, step_targets, step_inputs, scaled)
    gradient = own_rows(*step_terms(taken, taken_scaled, old_pieces))
    first_new = beta_one * first_moment[0] + (1.0 - beta_one) * gradient
    second_new = beta_two * second_moment[0] + (1.0 - beta_two) * gradient * gradient
    first_hat = first_new / (1.0 - beta_one**adam_step)
    second_hat = second_new / (1.0 - beta_two**adam_step)
    new_weights = old_weights - learn_rate * (
        first_hat / (jnp.sqrt(second_hat) + adam_eps) + decay_rate * old_weights
    )
    pieces = all_rows(arranged(b16(new_weights)))
    stacked = jnp.concatenate([b16(new_weights), b16(first_new), b16(second_new)], axis=0)
    moved = f32(migrated(stacked, owner_plan)).reshape((3, 1) + old_weights.shape)

    next_targets = slot_of(next_routes)
    own_next = to_chips(to_slots(next_targets, next_inputs))
    other_next = pass_on(own_next, "core", 1)
    met = serve(other_next, pieces)
    met = pass_on(met, "core", 1)
    partials = b16(f32(serve(own_next, pieces)) + f32(met))
    returned = exchange(partials.reshape(-1, CAP, D), "y").reshape(-1, D)
    chips_each = lax.axis_size("y") // EXPERTS
    slot = lax.broadcasted_iota(jnp.int32, (next_targets.shape[0], returned.shape[0]), 1)
    expert_slot = (slot // (chips_each * CAP)) * CAP + lax.rem(slot, CAP)
    picks = (next_targets[:, None] == expert_slot).astype(jnp.bfloat16)
    pair_sums = jnp.dot(picks, returned, preferred_element_type=jnp.float32)
    layer_output = b16(pair_sums * next_gates)
    return (layer_output, moved[0], moved[1], moved[2])


def solution(mesh):
    chips = mesh.devices.reshape(4, -1, mesh.shape["expert"] // 2, 2)
    tokens = P(ALL, None)
    slabs = P(EXPERT, DP, None)
    return jax.shard_map(
        whole_step,
        mesh=Mesh(chips, ALL),
        in_specs=(tokens,) * 7 + (slabs,) * 3 + (P(),),
        out_specs=(tokens,) + (slabs,) * 3,
        check_vma=False,
    )
```

```python
import jax
import jax.numpy as jnp
from jax import lax
from jax.experimental import pallas as pl
from jax.experimental.pallas import tpu as pltpu
from jax.sharding import Mesh
from jax.sharding import PartitionSpec as P

D = 2048
HID = 1152
EXPERTS = 4
CAP = 40
SLOTS = EXPERTS * CAP
DP = ("x", "z")
EXPERT = ("y", "core")
ALL = DP + EXPERT
WIDTH = 288
MAIN = 256
TAIL = WIDTH - MAIN
LEAD = 2 * MAIN
SIDE = 128 + MAIN
COLS = LEAD + SIDE
IN_SCALE = 2048 ** (-0.5)
OUT_SCALE = HID ** (-0.5)
TEST = False


beta_one = 0.9
beta_two = 0.95
learn_rate = 0.2
decay_rate = 0.1
adam_step = 10.0
adam_eps = 1e-08


def pass_on(value, axis, by):
    size = lax.axis_size(axis)
    return lax.ppermute(value, axis, [(k, (k + by) % size) for k in range(size)])


def exchange(value, axis):
    return lax.all_to_all(value, axis, split_axis=0, concat_axis=0, tiled=True)


def f32(value):
    return value.astype(jnp.float32)


def b16(value):
    return value.astype(jnp.bfloat16)


def slot_of(routes):
    ids = routes.reshape(-1)
    one_hot = ids[:, None] == jnp.arange(EXPERTS, dtype=jnp.int32)[None, :]
    count = ids.shape[0]
    before = lax.broadcasted_iota(jnp.int32, (count, count), 1) < lax.broadcasted_iota(
        jnp.int32, (count, count), 0
    )
    earlier = jnp.dot(
        before.astype(jnp.bfloat16),
        one_hot.astype(jnp.bfloat16),
        preferred_element_type=jnp.float32,
    )
    slots = jnp.sum(jnp.where(one_hot, earlier, 0.0), axis=1).astype(jnp.int32)
    return ids * CAP + slots


def to_slots(targets, payload):
    rows = lax.broadcasted_iota(jnp.int32, (SLOTS, targets.shape[0]), 0)
    selector = (rows == targets[None, :]).astype(jnp.bfloat16)
    filled = jnp.dot(selector, payload, preferred_element_type=jnp.float32)
    return filled.astype(jnp.bfloat16).reshape(EXPERTS, CAP, payload.shape[1])


def after(value, other):
    one = other[(0,) * other.ndim]
    return value + (one != one).astype(value.dtype)


def to_chips(slots):
    chips = lax.axis_size("y")
    return exchange(jnp.repeat(slots, chips // EXPERTS, axis=0), "y").reshape(-1, D)


def arranged(value):
    gate, up, down = (value[:, k * WIDTH : (k + 1) * WIDTH] for k in range(3))
    spare = jnp.zeros((value.shape[0], 128 - 3 * TAIL), value.dtype)
    tails = [gate[:, MAIN:], up[:, MAIN:], down[:, MAIN:], spare]
    return jnp.concatenate([gate[:, :MAIN], up[:, :MAIN]] + tails + [down[:, :MAIN]], axis=1)


def in_place(value):
    parts = []
    for k, start in enumerate((0, MAIN, LEAD + 128)):
        at = LEAD + k * TAIL
        parts += [value[:, start : start + MAIN], value[:, at : at + TAIL]]
    return jnp.concatenate(parts, axis=1)


def own_rows(terms):
    size_z, size_x, rows, columns = terms.shape
    flat = terms.reshape(size_z * size_x * rows, columns)
    half = lax.psum_scatter(flat, "z", scatter_dimension=0, tiled=True)
    parts = exchange(half.reshape(size_x, rows, columns), "x")
    return in_place(jnp.sum(f32(parts), axis=0))


def all_rows(value):
    size = lax.axis_size("x")
    wide = exchange(jnp.broadcast_to(value[None], (size,) + value.shape), "x")
    return lax.all_gather(wide, "z", axis=0)


def dot(a, b, dims=((1,), (0,))):
    return lax.dot_general(a, b, (dims, ((), ())), preferred_element_type=jnp.float32)


def lanes(shape):
    return lax.broadcasted_iota(jnp.int32, shape, 1)


def in_row_order(w, wn):
    size_z, size_x, rows, columns = w.shape
    wide = size_z * rows
    for k in range(size_x):
        wn[k * wide : (k + 1) * wide, :] = w[:, k].reshape(wide, columns)
    return wide


def back_terms(gate, up, down_back):
    sigmoid_gate = jax.nn.sigmoid(gate)
    silu_gate = gate * sigmoid_gate
    return (
        silu_gate * up,
        down_back * up * sigmoid_gate * (1.0 + gate * (1.0 - sigmoid_gate)),
        down_back * silu_gate,
    )


def terms_body(own_in, other_in, own_sc, other_sc, w, out, wn, pre, dn, g_in, g_sc):
    wide = in_row_order(w, wn)
    half = own_in.shape[0]
    count = 2 * half
    for at, rows_in, rows_sc in ((0, own_in, own_sc), (half, other_in, other_sc)):
        pre[at : at + half, :] = dot(rows_in[...], wn[:, : LEAD + 128]) * IN_SCALE
        dn[at : at + half, :] = dot(rows_sc[...], wn[:, LEAD:]) * OUT_SCALE

    def chunk(i, carry):
        at = pl.ds(pl.multiple_of(i * 64, 64), 64)
        act, gate_grad, up_grad = back_terms(pre[at, :MAIN], pre[at, MAIN:LEAD], dn[at, 128:])
        tail, down_tail = pre[at, LEAD:], dn[at, :128]
        lane = lanes(tail.shape)
        act_t, gate_t, up_t = back_terms(
            tail, pltpu.roll(tail, 128 - TAIL, 1), pltpu.roll(down_tail, 128 - 2 * TAIL, 1)
        )
        up_t = jnp.where(lane < 2 * TAIL, pltpu.roll(up_t, TAIL, 1), 0.0)
        here = (lane >= 2 * TAIL) & (lane < 3 * TAIL)
        g_in[at, :MAIN] = b16(gate_grad)
        g_in[at, MAIN:LEAD] = b16(up_grad)
        g_in[at, LEAD:] = b16(jnp.where(lane < TAIL, gate_t, up_t))
        g_sc[at, :128] = b16(jnp.where(here, pltpu.roll(act_t, 2 * TAIL, 1), 0.0))
        g_sc[at, 128:] = b16(act)
        return carry

    lax.fori_loop(0, count // 64, chunk, 0)
    over_rows = ((0,), (0,))
    size_z, size_x, rows, _ = w.shape
    for k in range(size_x):
        cols = slice(k * wide, (k + 1) * wide)
        a = dot(own_in[:, cols], g_in[:half, :], over_rows)
        a = (a + dot(other_in[:, cols], g_in[half:, :], over_rows)) * IN_SCALE
        b = dot(own_sc[:, cols], g_sc[:half, :], over_rows)
        b = (b + dot(other_sc[:, cols], g_sc[half:, :], over_rows)) * OUT_SCALE
        parts = (
            (slice(0, LEAD), b16(a[:, :LEAD])),
            (slice(LEAD, LEAD + 128), b16(a[:, LEAD:] + b[:, :128])),
            (slice(LEAD + 128, COLS), b16(b[:, 128:])),
        )
        for at, value in parts:
            out[:, k, :, at] = value.reshape(size_z, rows, value.shape[1])


def step_terms(own_in, other_in, own_sc, other_sc, w):
    count = 2 * own_in.shape[0]
    return pl.pallas_call(
        terms_body,
        out_shape=jax.ShapeDtypeStruct(w.shape, jnp.bfloat16),
        scratch_shapes=[
            pltpu.VMEM((D, COLS), jnp.bfloat16),
            pltpu.VMEM((count, LEAD + 128), jnp.float32),
            pltpu.VMEM((count, SIDE), jnp.float32),
            pltpu.VMEM((count, LEAD + 128), jnp.bfloat16),
            pltpu.VMEM((count, SIDE), jnp.bfloat16),
        ],
        interpret=TEST,
        name="step_terms",
    )(own_in, other_in, own_sc, other_sc, w)


def serve_body(taken, w, out, wn, pre, act):
    wide = in_row_order(w, wn)
    pre[...] = dot(taken[...], wn[:, : LEAD + 128]) * IN_SCALE

    def chunk(i, carry):
        at = pl.ds(pl.multiple_of(i * 64, 64), 64)
        gate, up = pre[at, :MAIN], pre[at, MAIN:LEAD]
        tail = pre[at, LEAD:]
        lane = lanes(tail.shape)
        act_t = tail * jax.nn.sigmoid(tail) * pltpu.roll(tail, 128 - TAIL, 1)
        here = (lane >= 2 * TAIL) & (lane < 3 * TAIL)
        act[at, :128] = b16(jnp.where(here, pltpu.roll(act_t, 2 * TAIL, 1), 0.0))
        act[at, 128:] = b16(gate * jax.nn.sigmoid(gate) * up)
        return carry

    lax.fori_loop(0, taken.shape[0] // 64, chunk, 0)
    for k in range(w.shape[1]):
        cols = slice(k * wide, (k + 1) * wide)
        total = dot(act[...], wn[cols, LEAD:], ((1,), (1,)))
        out[:, cols] = b16(total * OUT_SCALE)


def serve(taken, w):
    return pl.pallas_call(
        serve_body,
        out_shape=jax.ShapeDtypeStruct(taken.shape, jnp.bfloat16),
        scratch_shapes=[
            pltpu.VMEM((D, COLS), jnp.bfloat16),
            pltpu.VMEM((taken.shape[0], LEAD + 128), jnp.float32),
            pltpu.VMEM((taken.shape[0], SIDE), jnp.bfloat16),
        ],
        interpret=TEST,
        name="serve",
    )(taken, w)


def migrated(stacked, owner_plan):
    groups = lax.axis_size(EXPERT)
    positions = jnp.arange(groups, dtype=jnp.int32)
    goes = owner_plan[None, :] == positions[:, None]
    holder = jnp.sum(jnp.where(goes, positions[None, :], 0), axis=1)
    pieces = stacked.reshape(groups, -1, stacked.shape[1])
    spread = exchange(pieces, EXPERT)
    ordered = jnp.take(spread, holder, axis=0)
    return exchange(ordered, EXPERT).reshape(stacked.shape)


def whole_step(
    step_inputs,
    step_cotangent,
    step_routes,
    step_gates,
    next_inputs,
    next_routes,
    next_gates,
    master_weights,
    first_moment,
    second_moment,
    owner_plan,
):
    old_weights = master_weights[0]
    step_targets = slot_of(step_routes)
    scaled = b16(f32(step_cotangent) * step_gates)
    parts = lax.all_gather(arranged(b16(old_weights)), "x", axis=0)
    weights = lax.all_gather(parts, "z", axis=0)
    own_in = to_chips(to_slots(step_targets, step_inputs))
    own_sc = to_chips(to_slots(step_targets, scaled))
    other_in = pass_on(own_in, "core", 1)
    other_sc = pass_on(own_sc, "core", 1)
    gradient = own_rows(step_terms(own_in, other_in, own_sc, other_sc, weights))
    first_new = beta_one * first_moment[0] + (1.0 - beta_one) * gradient
    second_new = beta_two * second_moment[0] + (1.0 - beta_two) * gradient * gradient
    first_hat = first_new / (1.0 - beta_one**adam_step)
    second_hat = second_new / (1.0 - beta_two**adam_step)
    new_weights = old_weights - learn_rate * (
        first_hat / (jnp.sqrt(second_hat) + adam_eps) + decay_rate * old_weights
    )
    pieces = all_rows(arranged(b16(new_weights)))
    stacked = jnp.concatenate([b16(new_weights), b16(first_new), b16(second_new)], axis=0)
    moved = f32(migrated(stacked, owner_plan)).reshape((3, 1) + old_weights.shape)

    next_targets = slot_of(next_routes)
    next_slots = to_slots(after(next_targets, other_in), next_inputs)
    own_next = to_chips(next_slots)
    other_next = pass_on(own_next, "core", 1)
    met = serve(other_next, pieces)
    met = pass_on(met, "core", 1)
    partials = b16(f32(serve(own_next, pieces)) + f32(met))
    returned = exchange(partials.reshape(-1, CAP, D), "y").reshape(-1, D)
    chips_each = lax.axis_size("y") // EXPERTS
    slot = lax.broadcasted_iota(jnp.int32, (next_targets.shape[0], returned.shape[0]), 1)
    expert_slot = (slot // (chips_each * CAP)) * CAP + lax.rem(slot, CAP)
    picks = (next_targets[:, None] == expert_slot).astype(jnp.bfloat16)
    pair_sums = jnp.dot(picks, returned, preferred_element_type=jnp.float32)
    layer_output = b16(pair_sums * next_gates)
    return (layer_output, moved[0], moved[1], moved[2])


def solution(mesh):
    chips = mesh.devices.reshape(4, -1, mesh.shape["expert"] // 2, 2)
    tokens = P(ALL, None)
    slabs = P(EXPERT, DP, None)
    return jax.shard_map(
        whole_step,
        mesh=Mesh(chips, ALL),
        in_specs=(tokens,) * 7 + (slabs,) * 3 + (P(),),
        out_specs=(tokens,) + (slabs,) * 3,
        check_vma=False,
    )
```

```python
import jax
import jax.numpy as jnp
from jax import lax
from jax.experimental import pallas as pl
from jax.experimental.pallas import tpu as pltpu
from jax.sharding import Mesh
from jax.sharding import PartitionSpec as P

D = 2048
HID = 1152
EXPERTS = 4
CAP = 40
SLOTS = EXPERTS * CAP
DP = ("x", "z")
EXPERT = ("y", "core")
ALL = DP + EXPERT
WIDTH = 288
MAIN = 256
TAIL = WIDTH - MAIN
LEAD = 2 * MAIN
SIDE = 128 + MAIN
COLS = LEAD + SIDE
IN_SCALE = 2048 ** (-0.5)
OUT_SCALE = HID ** (-0.5)
TEST = False


beta_one = 0.9
beta_two = 0.95
learn_rate = 0.2
decay_rate = 0.1
adam_step = 10.0
adam_eps = 1e-08


def pass_on(value, axis, by):
    size = lax.axis_size(axis)
    return lax.ppermute(value, axis, [(k, (k + by) % size) for k in range(size)])


def exchange(value, axis):
    return lax.all_to_all(value, axis, split_axis=0, concat_axis=0, tiled=True)


def f32(value):
    return value.astype(jnp.float32)


def b16(value):
    return value.astype(jnp.bfloat16)


def slot_of(routes):
    ids = routes.reshape(-1)
    one_hot = ids[:, None] == jnp.arange(EXPERTS, dtype=jnp.int32)[None, :]
    count = ids.shape[0]
    before = lax.broadcasted_iota(jnp.int32, (count, count), 1) < lax.broadcasted_iota(
        jnp.int32, (count, count), 0
    )
    earlier = jnp.dot(
        before.astype(jnp.bfloat16),
        one_hot.astype(jnp.bfloat16),
        preferred_element_type=jnp.float32,
    )
    slots = jnp.sum(jnp.where(one_hot, earlier, 0.0), axis=1).astype(jnp.int32)
    return ids * CAP + slots


def to_slots(targets, payload):
    rows = lax.broadcasted_iota(jnp.int32, (SLOTS, targets.shape[0]), 0)
    selector = (rows == targets[None, :]).astype(jnp.bfloat16)
    filled = jnp.dot(selector, payload, preferred_element_type=jnp.float32)
    return filled.astype(jnp.bfloat16).reshape(EXPERTS, CAP, payload.shape[1])


def after(value, other):
    one = other[(0,) * other.ndim]
    return value + (one != one).astype(value.dtype)


def to_chips(slots):
    chips = lax.axis_size("y")
    return exchange(jnp.repeat(slots, chips // EXPERTS, axis=0), "y").reshape(-1, D)


def arranged(value):
    gate, up, down = (value[:, k * WIDTH : (k + 1) * WIDTH] for k in range(3))
    spare = jnp.zeros((value.shape[0], 128 - 3 * TAIL), value.dtype)
    tails = [gate[:, MAIN:], up[:, MAIN:], down[:, MAIN:], spare]
    return jnp.concatenate([gate[:, :MAIN], up[:, :MAIN]] + tails + [down[:, :MAIN]], axis=1)


def in_place(value):
    parts = []
    for k, start in enumerate((0, MAIN, LEAD + 128)):
        at = LEAD + k * TAIL
        parts += [value[:, start : start + MAIN], value[:, at : at + TAIL]]
    return jnp.concatenate(parts, axis=1)


def own_rows(terms):
    size_z, size_x, rows, columns = terms.shape
    flat = terms.reshape(size_z * size_x * rows, columns)
    half = lax.psum_scatter(flat, "z", scatter_dimension=0, tiled=True)
    parts = exchange(half.reshape(size_x, rows, columns), "x")
    return in_place(jnp.sum(f32(parts), axis=0))


def all_rows(value):
    size = lax.axis_size("x")
    wide = exchange(jnp.broadcast_to(value[None], (size,) + value.shape), "x")
    return lax.all_gather(wide, "z", axis=0)


def dot(a, b, dims=((1,), (0,))):
    return lax.dot_general(a, b, (dims, ((), ())), preferred_element_type=jnp.float32)


def lanes(shape):
    return lax.broadcasted_iota(jnp.int32, shape, 1)


def in_row_order(w, wn):
    size_z, size_x, rows, columns = w.shape
    wide = size_z * rows
    for k in range(size_x):
        wn[k * wide : (k + 1) * wide, :] = w[:, k].reshape(wide, columns)
    return wide


def back_terms(gate, up, down_back):
    sigmoid_gate = jax.nn.sigmoid(gate)
    silu_gate = gate * sigmoid_gate
    return (
        silu_gate * up,
        down_back * up * sigmoid_gate * (1.0 + gate * (1.0 - sigmoid_gate)),
        down_back * silu_gate,
    )


def terms_body(own_in, other_in, own_sc, other_sc, w, out, wn, pre, dn, g_in, g_sc):
    wide = in_row_order(w, wn)
    half = own_in.shape[0]
    count = 2 * half
    for at, rows_in, rows_sc in ((0, own_in, own_sc), (half, other_in, other_sc)):
        pre[at : at + half, :] = dot(rows_in[...], wn[:, : LEAD + 128]) * IN_SCALE
        dn[at : at + half, :] = dot(rows_sc[...], wn[:, LEAD:]) * OUT_SCALE

    def chunk(i, carry):
        at = pl.ds(pl.multiple_of(i * 64, 64), 64)
        act, gate_grad, up_grad = back_terms(pre[at, :MAIN], pre[at, MAIN:LEAD], dn[at, 128:])
        tail, down_tail = pre[at, LEAD:], dn[at, :128]
        lane = lanes(tail.shape)
        act_t, gate_t, up_t = back_terms(
            tail, pltpu.roll(tail, 128 - TAIL, 1), pltpu.roll(down_tail, 128 - 2 * TAIL, 1)
        )
        up_t = jnp.where(lane < 2 * TAIL, pltpu.roll(up_t, TAIL, 1), 0.0)
        here = (lane >= 2 * TAIL) & (lane < 3 * TAIL)
        g_in[at, :MAIN] = b16(gate_grad)
        g_in[at, MAIN:LEAD] = b16(up_grad)
        g_in[at, LEAD:] = b16(jnp.where(lane < TAIL, gate_t, up_t))
        g_sc[at, :128] = b16(jnp.where(here, pltpu.roll(act_t, 2 * TAIL, 1), 0.0))
        g_sc[at, 128:] = b16(act)
        return carry

    lax.fori_loop(0, count // 64, chunk, 0)
    over_rows = ((0,), (0,))
    size_z, size_x, rows, _ = w.shape
    for k in range(size_x):
        cols = slice(k * wide, (k + 1) * wide)
        a = dot(own_in[:, cols], g_in[:half, :], over_rows)
        a = (a + dot(other_in[:, cols], g_in[half:, :], over_rows)) * IN_SCALE
        b = dot(own_sc[:, cols], g_sc[:half, :], over_rows)
        b = (b + dot(other_sc[:, cols], g_sc[half:, :], over_rows)) * OUT_SCALE
        parts = (
            (slice(0, LEAD), b16(a[:, :LEAD])),
            (slice(LEAD, LEAD + 128), b16(a[:, LEAD:] + b[:, :128])),
            (slice(LEAD + 128, COLS), b16(b[:, 128:])),
        )
        for at, value in parts:
            out[:, k, :, at] = value.reshape(size_z, rows, value.shape[1])


def step_terms(own_in, other_in, own_sc, other_sc, w):
    count = 2 * own_in.shape[0]
    return pl.pallas_call(
        terms_body,
        out_shape=jax.ShapeDtypeStruct(w.shape, jnp.bfloat16),
        in_specs=[pl.BlockSpec(memory_space=pltpu.VMEM), pl.BlockSpec()] * 2 + [pl.BlockSpec()],
        compiler_params=pltpu.CompilerParams(vmem_limit_bytes=36 * 2**20),
        scratch_shapes=[
            pltpu.VMEM((D, COLS), jnp.bfloat16),
            pltpu.VMEM((count, LEAD + 128), jnp.float32),
            pltpu.VMEM((count, SIDE), jnp.float32),
            pltpu.VMEM((count, LEAD + 128), jnp.bfloat16),
            pltpu.VMEM((count, SIDE), jnp.bfloat16),
        ],
        interpret=TEST,
        name="step_terms",
    )(own_in, other_in, own_sc, other_sc, w)


def serve_body(taken, w, out, wn, pre, act):
    wide = in_row_order(w, wn)
    pre[...] = dot(taken[...], wn[:, : LEAD + 128]) * IN_SCALE

    def chunk(i, carry):
        at = pl.ds(pl.multiple_of(i * 64, 64), 64)
        gate, up = pre[at, :MAIN], pre[at, MAIN:LEAD]
        tail = pre[at, LEAD:]
        lane = lanes(tail.shape)
        act_t = tail * jax.nn.sigmoid(tail) * pltpu.roll(tail, 128 - TAIL, 1)
        here = (lane >= 2 * TAIL) & (lane < 3 * TAIL)
        act[at, :128] = b16(jnp.where(here, pltpu.roll(act_t, 2 * TAIL, 1), 0.0))
        act[at, 128:] = b16(gate * jax.nn.sigmoid(gate) * up)
        return carry

    lax.fori_loop(0, taken.shape[0] // 64, chunk, 0)
    for k in range(w.shape[1]):
        cols = slice(k * wide, (k + 1) * wide)
        total = dot(act[...], wn[cols, LEAD:], ((1,), (1,)))
        out[:, cols] = b16(total * OUT_SCALE)


def serve(taken, w):
    return pl.pallas_call(
        serve_body,
        out_shape=jax.ShapeDtypeStruct(taken.shape, jnp.bfloat16),
        in_specs=[pl.BlockSpec(memory_space=pltpu.VMEM)] * 2,
        out_specs=pl.BlockSpec(memory_space=pltpu.VMEM),
        compiler_params=pltpu.CompilerParams(vmem_limit_bytes=24 * 2**20),
        scratch_shapes=[
            pltpu.VMEM((D, COLS), jnp.bfloat16),
            pltpu.VMEM((taken.shape[0], LEAD + 128), jnp.float32),
            pltpu.VMEM((taken.shape[0], SIDE), jnp.bfloat16),
        ],
        interpret=TEST,
        name="serve",
    )(taken, w)


def migrated(stacked, owner_plan):
    groups = lax.axis_size(EXPERT)
    positions = jnp.arange(groups, dtype=jnp.int32)
    goes = owner_plan[None, :] == positions[:, None]
    holder = jnp.sum(jnp.where(goes, positions[None, :], 0), axis=1)
    pieces = stacked.reshape(groups, -1, stacked.shape[1])
    spread = exchange(pieces, EXPERT)
    ordered = jnp.take(spread, holder, axis=0)
    return exchange(ordered, EXPERT).reshape(stacked.shape)


def whole_step(
    step_inputs,
    step_cotangent,
    step_routes,
    step_gates,
    next_inputs,
    next_routes,
    next_gates,
    master_weights,
    first_moment,
    second_moment,
    owner_plan,
):
    old_weights = master_weights[0]
    step_targets = slot_of(step_routes)
    scaled = b16(f32(step_cotangent) * step_gates)
    parts = lax.all_gather(arranged(b16(old_weights)), "x", axis=0)
    weights = lax.all_gather(parts, "z", axis=0)
    own_in = to_chips(to_slots(step_targets, step_inputs))
    own_sc = to_chips(to_slots(step_targets, scaled))
    other_in = pass_on(own_in, "core", 1)
    other_sc = pass_on(own_sc, "core", 1)
    gradient = own_rows(step_terms(own_in, other_in, own_sc, other_sc, weights))
    first_new = beta_one * first_moment[0] + (1.0 - beta_one) * gradient
    second_new = beta_two * second_moment[0] + (1.0 - beta_two) * gradient * gradient
    first_hat = first_new / (1.0 - beta_one**adam_step)
    second_hat = second_new / (1.0 - beta_two**adam_step)
    new_weights = old_weights - learn_rate * (
        first_hat / (jnp.sqrt(second_hat) + adam_eps) + decay_rate * old_weights
    )
    pieces = all_rows(arranged(b16(new_weights)))
    stacked = jnp.concatenate([b16(new_weights), b16(first_new), b16(second_new)], axis=0)
    moved = f32(migrated(stacked, owner_plan)).reshape((3, 1) + old_weights.shape)

    next_targets = slot_of(next_routes)
    next_slots = to_slots(after(next_targets, other_in), next_inputs)
    own_next = to_chips(next_slots)
    other_next = pass_on(own_next, "core", 1)
    met = serve(other_next, pieces)
    met = pass_on(met, "core", 1)
    partials = b16(f32(serve(own_next, pieces)) + f32(met))
    returned = exchange(partials.reshape(-1, CAP, D), "y").reshape(-1, D)
    chips_each = lax.axis_size("y") // EXPERTS
    slot = lax.broadcasted_iota(jnp.int32, (next_targets.shape[0], returned.shape[0]), 1)
    expert_slot = (slot // (chips_each * CAP)) * CAP + lax.rem(slot, CAP)
    picks = (next_targets[:, None] == expert_slot).astype(jnp.bfloat16)
    pair_sums = jnp.dot(picks, returned, preferred_element_type=jnp.float32)
    layer_output = b16(pair_sums * next_gates)
    return (layer_output, moved[0], moved[1], moved[2])


def solution(mesh):
    chips = mesh.devices.reshape(4, -1, mesh.shape["expert"] // 2, 2)
    tokens = P(ALL, None)
    slabs = P(EXPERT, DP, None)
    return jax.shard_map(
        whole_step,
        mesh=Mesh(chips, ALL),
        in_specs=(tokens,) * 7 + (slabs,) * 3 + (P(),),
        out_specs=(tokens,) + (slabs,) * 3,
        check_vma=False,
    )
```
